32 devices in a mesh: section: 4 (over y, x), ctx: 4 (over z), tp: 2 (over core).
Axes of the slice: x: 2, y: 2, z: 4, core: 2. Of those that a mesh axis runs over, the one named last changes fastest.
Arguments:
- queries: bfloat16 [2048, 8, 8, 128], P('ctx', 'tp', 'section'), may hold values from -44 to 44
- key_states: bfloat16 [2048, 8, 128], P('ctx', 'tp'), may hold values from -4 to 4
- value_states: bfloat16 [2048, 8, 128], P('ctx', 'tp'), may hold values from -6 to 6
- out_grad: bfloat16 [2048, 8, 8, 128], P('ctx', 'tp', 'section'), may hold values from -6 to 6
- band_offsets: int32 [16, 3], replicated, may hold values from -1 to 4, as said below
- global_blocks: int32 [16, 4], replicated, may hold values from -1 to 8, as said below
Outputs:
- attended: bfloat16 [2048, 8, 8, 128], P('ctx', 'tp', 'section')
- query_grad: float32 [2048, 8, 8, 128], P('ctx', 'tp', 'section')
- key_grad: float32 [2048, 8, 128], P('ctx', 'tp')
- value_grad: float32 [2048, 8, 128], P('ctx', 'tp')
The draws below stay inside these ranges and needn't reach their ends.
Inputs may be any that keep to these rules, and one draw needn't show every extreme that they name: `band_offsets`: in every row r the first offset is 0, the second lies in 1 to 2 and the third in 3 to 4; an offset larger than r is replaced by -1. `global_blocks`: entry n of row r is either -1 or n * 4, and it is n * 4 only when n * 4 < r - 4.
All inputs are finite; a program needn't handle non-finite values.
Results may differ from the reference program's by a relative error of at most 0.017.
Values may be sent and summed in bfloat16 or wider, within the bound.
A program may use at most 128 MiB of HBM per device.

```python
import jax
import jax.numpy as jnp
from jax import lax

HD = 128
KVH = 8
GROUP = 8
BLK = 128
NBAND = 3
NGLOB = 4
L = 2048
QB_DEV = 4
NB = 16
GSTRIDE = 4


def make_keys(key):
    noise_key = jax.random.fold_in(key, 101)
    base = jnp.clip(jax.random.normal(noise_key, (L, KVH, HD), jnp.float32), -4.0, 4.0)
    return base


def draw_key_states(key, part):
    return make_keys(key).astype(jnp.bfloat16)


def draw_queries(key, part):
    base = jnp.clip(jax.random.normal(jax.random.fold_in(key, 105), (L, KVH, GROUP, HD), jnp.float32), -4.0, 4.0)
    return base.astype(jnp.bfloat16)


def draw_band_offsets(key, part):
    row_ids = jnp.arange(NB, dtype=jnp.int32)[:, None]
    half_reach = QB_DEV // 2
    second = jax.random.randint(jax.random.fold_in(key, 201), (NB, 1), 1, half_reach + 1)
    third = jax.random.randint(jax.random.fold_in(key, 202), (NB, 1), half_reach + 1, QB_DEV + 1)
    third = jnp.where(row_ids == NB - 1, QB_DEV, third)
    offsets = jnp.concatenate([jnp.zeros((NB, 1), jnp.int32), second, third], axis=1)
    return jnp.where(offsets <= row_ids, offsets, -1).astype(jnp.int32)


def draw_global_blocks(key, part):
    row_ids = jnp.arange(NB, dtype=jnp.int32)[:, None]
    blocks = jnp.arange(NGLOB, dtype=jnp.int32)[None, :] * GSTRIDE
    keeping = jax.random.randint(jax.random.fold_in(key, 301), (NB, NGLOB), 0, 4) < 3
    keeping = keeping | (row_ids == NB - 1)
    eligible = blocks < row_ids - QB_DEV
    return jnp.where(eligible & keeping, blocks, -1).astype(jnp.int32)


def level_of(own_key, shape, split, low, top_value):
    factor_of = 1.0
    for dim, shards_of in split:
        steps = jax.random.uniform(jax.random.fold_in(jax.random.fold_in(own_key, 6), dim), (shards_of,), jnp.float32, low / len(split), top_value / len(split))
        factor_of = factor_of * jnp.repeat(jnp.exp(steps), shape[dim] // shards_of).reshape((-1,) + (1,) * (len(shape) - 1 - dim))
    return factor_of


def normal_values(stream_key, dims, deviation, bound, cuts=(), held_as=jnp.bfloat16):
    result = jax.random.normal(stream_key, dims, jnp.float32) * deviation
    if len(cuts) > 0:
        result = level_of(stream_key, dims, cuts, -0.22, 0.18) * result
    return jnp.clip(result, min=-bound, max=bound).astype(held_as)


def setup_inputs(seed: int = 0) -> dict:
    keys = jax.random.split(jax.random.key(seed), 7)
    return {
        "queries": draw_queries(jax.random.fold_in(keys[6], 71), 0),
        "key_states": draw_key_states(jax.random.fold_in(keys[6], 71), 0),
        "value_states": normal_values(keys[2], (L, KVH, HD), 1.0, 6.0, ((0, 4), (1, 2))),
        "out_grad": normal_values(keys[3], (L, KVH, GROUP, HD), 1.0, 6.0, ((0, 4), (1, 2), (2, 4))),
        "band_offsets": draw_band_offsets(jax.random.fold_in(keys[6], 71), 0),
        "global_blocks": draw_global_blocks(jax.random.fold_in(keys[6], 71), 0),
    }


def block_lists(band_offsets, global_blocks):
    row_ids = jnp.arange(band_offsets.shape[0], dtype=jnp.int32)[:, None]
    band_ids = row_ids - band_offsets
    chosen = jnp.concatenate([band_ids, global_blocks], axis=1)
    usable = jnp.concatenate([band_offsets >= 0, global_blocks >= 0], axis=1)
    return jnp.where(usable, chosen, 0).astype(jnp.int32), usable


def reference(queries, key_states, value_states, out_grad, band_offsets, global_blocks):
    scale_factor = HD ** -0.5
    block_ids, usable = block_lists(band_offsets, global_blocks)
    query_blocks = queries.reshape(NB, BLK, KVH, GROUP, HD)
    grad_blocks = out_grad.reshape(NB, BLK, KVH, GROUP, HD)
    key_blocks = key_states.reshape(NB, BLK, KVH, HD)
    value_blocks = value_states.reshape(NB, BLK, KVH, HD)
    lower_half = jnp.arange(BLK)[:, None] >= jnp.arange(BLK)[None, :]
    first_slot = jnp.arange(NBAND + NGLOB) == 0

    def step_row(running, inputs):
        key_acc, value_acc = running
        row_ids, row_ok, query_row, grad_row = inputs
        key_sel = key_blocks[row_ids].astype(jnp.float32)
        value_sel = value_blocks[row_ids].astype(jnp.float32)
        query_wide = query_row.astype(jnp.float32)
        grad_wide = grad_row.astype(jnp.float32)
        scores = jnp.einsum('ihgd,njhd->hginj', query_wide, key_sel) * scale_factor
        reach = jnp.logical_not(first_slot)[None, :, None] | lower_half[:, None, :]
        allowed = row_ok[None, :, None] & reach
        scores = jnp.where(allowed, scores, -jnp.inf)
        row_top = jnp.max(scores, axis=(3, 4), keepdims=True)
        row_total = jnp.sum(jnp.exp(scores - row_top), axis=(3, 4), keepdims=True)
        log_total = row_top + jnp.log(row_total)
        weights = jnp.exp(scores - log_total)
        weights_low = weights.astype(jnp.bfloat16)
        low_wide = weights_low.astype(jnp.float32)
        attended = jnp.einsum('hginj,njhd->ihgd', low_wide, value_sel).astype(jnp.bfloat16)
        row_dots = jnp.sum(grad_wide * attended.astype(jnp.float32), axis=-1)
        dweights = jnp.einsum('ihgd,njhd->hginj', grad_wide, value_sel)
        dscores = (weights * (dweights - jnp.transpose(row_dots, (1, 2, 0))[..., None, None])).astype(jnp.bfloat16)
        dscore_wide = dscores.astype(jnp.float32)
        query_grad = scale_factor * jnp.einsum('hginj,njhd->ihgd', dscore_wide, key_sel)
        key_part = scale_factor * jnp.einsum('hginj,ihgd->njhd', dscore_wide, query_wide)
        value_part = jnp.einsum('hginj,ihgd->njhd', low_wide, grad_wide)
        key_acc = key_acc.at[row_ids].add(key_part)
        value_acc = value_acc.at[row_ids].add(value_part)
        return (key_acc, value_acc), (attended, query_grad)

    empty_grads = jnp.zeros((NB, BLK, KVH, HD), jnp.float32)
    (key_acc, value_acc), (attended, query_grad) = lax.scan(
        step_row, (empty_grads, empty_grads), (block_ids, usable, query_blocks, grad_blocks))
    return (attended.reshape(L, KVH, GROUP, HD), query_grad.reshape(L, KVH, GROUP, HD),
            key_acc.reshape(L, KVH, HD), value_acc.reshape(L, KVH, HD))
```

```python
import functools

import jax
import jax.numpy as jnp
from jax import lax
from jax.experimental import pallas as pl
from jax.experimental.pallas import tpu as pltpu
from jax.sharding import PartitionSpec as P

BLK = 128
NBAND = 3
NGLOB = 4
REACH = ((1, 2), (3, 4))
LOG2E = 1.4426950408889634
LOW = -1e30


def global_count(all_blocks, stride_blocks, own_blocks):
    return len([n for n in range(NGLOB) if n * stride_blocks < all_blocks - 1 - own_blocks])


def dot_nt(a, b):
    return lax.dot_general(a, b, (((1,), (1,)), ((), ())), preferred_element_type=jnp.float32)


def dot_tn(a, b):
    return lax.dot_general(a, b, (((0,), (0,)), ((), ())), preferred_element_type=jnp.float32)


def dot_nn(a, b):
    return lax.dot_general(a, b, (((1,), (0,)), ((), ())), preferred_element_type=jnp.float32)


def head_rows(own_blocks, n_glob, scale, row_base, band_ref, glob_ref, q_of, g_of, key_of, value_of,
              put_att, put_dq, add_key, add_value, rows):
    for i in rows:
        row = row_base + i
        offs = [band_ref[1 + m, row] for m in range(NBAND - 1)]
        chosen = [glob_ref[n, row] for n in range(n_glob)]
        q, g = q_of(i), g_of(i)

        def selected(block_of):
            parts = [block_of(own_blocks + i)]
            for m in range(NBAND - 1):
                near, far = REACH[m]
                parts.append(jnp.where(offs[m] == near, block_of(own_blocks + i - near),
                                       block_of(own_blocks + i - far)))
            for n in range(n_glob):
                parts.append(block_of(2 * own_blocks + n))
            return jnp.concatenate(parts, axis=0)

        keys, values = selected(key_of), selected(value_of)
        scores = dot_nt(keys, q)
        width = scores.shape[1]
        key_pos = lax.broadcasted_iota(jnp.int32, (BLK, width), 0)
        query_pos = lax.broadcasted_iota(jnp.int32, (BLK, width), 1) % BLK
        usable = [o >= 0 for o in offs] + [c >= 0 for c in chosen]
        pieces = [jnp.where(key_pos <= query_pos, scores[:BLK], LOW)]
        for n, ok in enumerate(usable):
            pieces.append(scores[(n + 1) * BLK:(n + 2) * BLK] + jnp.where(ok, 0.0, LOW))
        scores = jnp.concatenate(pieces, axis=0)
        top = jnp.max(scores, axis=0, keepdims=True)
        probs = jnp.exp2((scores - top) * (scale * LOG2E))
        weights = probs * (1.0 / jnp.sum(probs, axis=0, keepdims=True))
        low = weights.astype(jnp.bfloat16)
        att = dot_tn(values, low).astype(jnp.bfloat16).astype(jnp.float32)
        put_att(i, att.T)
        dots = jnp.sum(g.astype(jnp.float32).T * att, axis=0, keepdims=True)
        ds = (weights * (dot_nt(values, g) - dots)).astype(jnp.bfloat16)
        put_dq(i, (dot_tn(keys, ds) * scale).T)
        dk, dv = dot_nn(ds, q) * scale, dot_nn(low, g)
        for part, add in ((dk, add_key), (dv, add_value)):
            add(own_blocks + i, part[:BLK])
            for m in range(NBAND - 1):
                piece = part[(m + 1) * BLK:(m + 2) * BLK]
                for off in REACH[m]:
                    add(own_blocks + i - off, jnp.where(offs[m] == off, piece, 0.0))
            for n in range(n_glob):
                at = (NBAND + n) * BLK
                add(2 * own_blocks + n, part[at:at + BLK])


def fused_kernel(own, n_glob, owner_step, ctx_count, bits, scale, group, band_hbm, glob_hbm, q_hbm, g_hbm,
                 key_hbm, value_hbm, att_ref, dq_ref, dkey_ref, dvalue_ref,
                 band_ref, glob_ref, q_ref, g_ref, kv_in, load_s, kv_wide, kv_ref, q_wide, g_wide, att_wide, out_ref, seen, acc, acc_own, parts, paired, halves, returned, farback, totals, swapped,
                 near_s, near_r, far_s, far_r, pair_s, pair_r, farpair_s, farpair_r,
                 one_s, one_r, own_s, own_r, farone_s, farone_r, back_s, back_r, farback_s, farback_r,
                 two_s, two_r, three_s, three_r):
    heads, dim = kv_ref.shape[1], kv_ref.shape[-1]
    tok, lanes = own * BLK, heads * group

    loads = [pltpu.make_async_copy(src, dst, load_s.at[n]) for n, (src, dst) in enumerate((
        (key_hbm, kv_in.at[0]), (value_hbm, kv_in.at[1]), (q_hbm, q_ref), (g_hbm, g_ref),
        (band_hbm, band_ref), (glob_hbm, glob_ref)))]
    for load in loads:
        load.start()
    p, s, parity = lax.axis_index("ctx"), lax.axis_index("section"), lax.axis_index("tp") % 2

    def other(j):
        bit = (1 << (j % bits)) * (1 - parity) + (1 << ((j + 1) % bits)) * parity
        side = (s // bit) % 2
        return s + bit * (1 - 2 * side), side

    mate, role = other(0)
    has_prev, has_next = p > 0, p < ctx_count - 1
    index = p // owner_step

    def owns(at):
        return jnp.logical_and(at % owner_step == 0, at // owner_step < n_glob)

    def sends_far(d):
        return jnp.logical_and(owns(p), p + d < ctx_count)

    def gets_far(d):
        return jnp.logical_and(p - d >= 0, owns(p - d + (p - d < 0) * ctx_count * owner_step))

    spans = range(2, ctx_count)

    def is_far(n):
        return p >= n * owner_step + 2

    def is_next(n):
        return p == n * owner_step + 1

    def copy(src, dst, ss, rs, axis, to):
        return pltpu.make_async_remote_copy(src_ref=src, dst_ref=dst, send_sem=ss, recv_sem=rs,
                                            device_id={axis: to}, device_id_type=pl.DeviceIdType.MESH)

    bar = pltpu.get_barrier_semaphore()
    links = [(has_prev, "ctx", p - 1), (has_next, "ctx", p + 1)]
    for d in spans:
        links += [(sends_far(d), "ctx", p + d), (gets_far(d), "ctx", p - d)]
    for j in range(bits):
        pl.semaphore_signal(bar, inc=1, device_id={"section": other(j)[0]}, device_id_type=pl.DeviceIdType.MESH)
    for cond, axis, to in links:
        @pl.when(cond)
        def _(axis=axis, to=to):
            pl.semaphore_signal(bar, inc=1, device_id={axis: to}, device_id_type=pl.DeviceIdType.MESH)
    peers = bits
    for cond, _, _ in links:
        peers = peers + jnp.where(cond, 1, 0)
    for which in range(2):
        loads[which].wait()
        kv_wide[...] = kv_in[which].astype(jnp.float32)
        for h in range(heads):
            kv_ref[which, h] = kv_wide[pl.ds(h, tok, stride=heads), :].astype(kv_ref.dtype).reshape(own, BLK, dim)
    pl.semaphore_wait(bar, peers)

    def near_copy(h):
        return copy(kv_ref.at[role, h], seen.at[role, h, pl.ds(0, own)], near_s.at[h], near_r.at[h], "ctx", p + 1)

    def far_copy(h, d):
        return copy(kv_ref.at[role, h, 0], seen.at[role, h, own + index], far_s.at[h, d], far_r.at[h, index],
                    "ctx", p + d)

    def far_arrival(h, n):
        return copy(kv_ref.at[role, h, 0], seen.at[role, h, own + n], far_s.at[h, 0], far_r.at[h, n], "ctx", p)

    def pair_copy(h, half):
        blocks = seen.at[half, h, pl.ds(0, own)]
        return copy(blocks, blocks, pair_s.at[h], pair_r.at[h], "section", mate)

    def farpair_copy(h, n, half):
        block = seen.at[half, h, own + n]
        return copy(block, block, farpair_s.at[h, n], farpair_r.at[h, n], "section", mate)

    def one_copy(h, src_half):
        return copy(parts.at[src_half, h, pl.ds(0, own)], paired.at[h, pl.ds(0, own)],
                    one_s.at[h], one_r.at[h], "section", mate)

    def own_copy(h, src_half):
        return copy(parts.at[src_half, h, pl.ds(own, own)], paired.at[h, pl.ds(own, own)],
                    own_s.at[h], own_r.at[h], "section", mate)

    def farone_copy(h, n, src_half):
        return copy(parts.at[src_half, h, 2 * own + n], paired.at[h, 2 * own + n],
                    farone_s.at[h, n], farone_r.at[h, n], "section", mate)

    def back_copy(h):
        return copy(halves.at[h, pl.ds(0, own)], returned.at[h], back_s.at[h], back_r.at[h], "ctx", p - 1)

    def farback_copy(h, n):
        return copy(halves.at[h, 2 * own + n], farback.at[h, p - n * owner_step], farback_s.at[h, n],
                    farback_r.at[h, p - n * owner_step], "ctx", n * owner_step)

    def farback_arrival(h, d):
        return copy(halves.at[h, 2 * own], farback.at[h, d], farback_s.at[h, 0], farback_r.at[h, d], "ctx", p)

    def two_copy(h, j):
        return copy(totals.at[j, h], swapped.at[j, h], two_s.at[j, h], two_r.at[j, h], "section", other(j)[0])

    def three_copy(h, half):
        return copy(out_ref.at[half, h], out_ref.at[half, h], three_s.at[h], three_r.at[h], "section", mate)

    for h in range(heads):
        @pl.when(has_next)
        def _(h=h):
            near_copy(h).start()
        for d in spans:
            @pl.when(sends_far(d))
            def _(h=h, d=d):
                far_copy(h, d).start()

    @pl.when(jnp.logical_not(has_prev))
    def _():
        seen[:, :, :own] = jnp.zeros_like(seen[:, :, :own])
    for n in range(n_glob):
        @pl.when(p < n * owner_step + 1)
        def _(n=n):
            seen[:, :, own + n] = jnp.zeros_like(seen[:, :, own + n])

    def pass_on(h):
        @pl.when(has_prev)
        def _():
            near_copy(h).wait_recv()
            pair_copy(h, role).start()
        for n in range(n_glob):
            @pl.when(is_far(n))
            def _(n=n):
                far_arrival(h, n).wait_recv()
                farpair_copy(h, n, role).start()

    def arrived(h):
        @pl.when(has_prev)
        def _():
            pair_copy(h, 1 - role).wait_recv()
        for n in range(n_glob):
            @pl.when(is_far(n))
            def _(n=n):
                farpair_copy(h, n, 1 - role).wait_recv()

            @pl.when(is_next(n))
            def _(n=n):
                seen[:, h, own + n] = seen[:, h, 0]

    touched = set()

    def add_to(which):
        def add(slot, part):
            if (which, slot) in touched:
                acc[which, slot] += part
            else:
                acc[which, slot] = part
                touched.add((which, slot))
        return add

    def block_of(which, h):
        def get(slot):
            if slot < own:
                return seen[which, h, slot]
            if slot < 2 * own:
                return kv_ref[which, h, slot - own]
            return seen[which, h, slot - own]
        return get

    def compute(h, rows):
        def spots(i):
            return [pl.ds(i * BLK * lanes + h * group + n, BLK, stride=lanes) for n in range(group)]

        def rows_of(ref, i):
            return jnp.concatenate([ref[at, :] for at in spots(i)], axis=0).astype(jnp.bfloat16)

        def put_att(i, x):
            for n, at in enumerate(spots(i)):
                att_wide[at, :] = x[n * BLK:(n + 1) * BLK]

        def put_dq(i, x):
            for n, at in enumerate(spots(i)):
                dq_ref[at, :] = x[n * BLK:(n + 1) * BLK]

        head_rows(own, n_glob, scale, p * own, band_ref, glob_ref, lambda i: rows_of(q_wide, i), lambda i: rows_of(g_wide, i),
                  block_of(0, h), block_of(1, h), put_att, put_dq, add_to(0), add_to(1), rows)

    def send_parts(h):
        for n in range(n_glob):
            @pl.when(is_next(n))
            def _(n=n):
                acc[:, 0] += acc[:, 2 * own + n]
        parts[:, h] = acc[...].astype(parts.dtype)
        one_copy(h, 1 - role).start()
        for n in range(n_glob):
            @pl.when(is_far(n))
            def _(n=n):
                farone_copy(h, n, 1 - role).start()
        own_copy(h, 1 - role).start()

    def wide(x):
        return x.astype(jnp.float32)

    def send_back(h):
        one_copy(h, role).wait_recv()
        both = pl.ds(0, own)
        halves[h, both] = (wide(parts[role, h, both]) + wide(paired[h, both])).astype(halves.dtype)

        @pl.when(has_prev)
        def _():
            back_copy(h).start()
        for n in range(n_glob):
            @pl.when(is_far(n))
            def _(n=n):
                farone_copy(h, n, role).wait_recv()
                at = 2 * own + n
                halves[h, at] = (wide(parts[role, h, at]) + wide(paired[h, at])).astype(halves.dtype)
                farback_copy(h, n).start()
        own_copy(h, role).wait_recv()
        mine = pl.ds(own, own)
        halves[h, mine] = (wide(parts[role, h, mine]) + wide(paired[h, mine])).astype(halves.dtype)

    def swap(h):
        mine = pl.ds(own, own)
        total = acc_own
        total[...] = wide(halves[h, mine])

        @pl.when(has_next)
        def _():
            back_copy(h).wait_recv()
            total[...] += wide(returned[h])
        for d in spans:
            @pl.when(sends_far(d))
            def _(d=d):
                farback_arrival(h, d).wait_recv()
                total[0] += wide(farback[h, d])
        totals[1, h] = total[...].astype(totals.dtype)
        two_copy(h, 1).start()

    def spread(h):
        for j in range(1, bits):
            two_copy(h, j).wait_recv()
            result = (wide(totals[j, h]) + wide(swapped[j, h])).astype(totals.dtype)
            if j + 1 < bits:
                totals[j + 1, h] = result
                two_copy(h, j + 1).start()
            else:
                out_ref[role, h] = result
        three_copy(h, role).start()

    for load in loads[2:]:
        load.wait()
    q_wide[...] = q_ref[...].astype(jnp.float32)
    g_wide[...] = g_ref[...].astype(jnp.float32)
    pass_on(0)

    def step(h, carry):
        @pl.when(h >= 3)
        def _():
            spread(h - 3)

        @pl.when(jnp.logical_and(h >= 2, h < heads + 2))
        def _():
            swap(h - 2)

        @pl.when(h < heads)
        def _():
            arrived(h)
            compute(h, range(own // 2))

        @pl.when(h + 1 < heads)
        def _():
            pass_on(h + 1)

        @pl.when(h == heads)
        def _():
            att_ref[...] = att_wide[...].astype(att_ref.dtype)

        @pl.when(jnp.logical_and(h >= 1, h < heads + 1))
        def _():
            send_back(h - 1)

        @pl.when(h < heads)
        def _():
            compute(h, range(own // 2, own))
            send_parts(h)
        return carry

    lax.fori_loop(0, heads + 3, step, 0)

    def finish(h, carry):
        @pl.when(has_next)
        def _():
            near_copy(h).wait_send()
        for d in spans:
            @pl.when(sends_far(d))
            def _(d=d):
                far_copy(h, d).wait_send()

        @pl.when(has_prev)
        def _():
            pair_copy(h, role).wait_send()
            back_copy(h).wait_send()
        one_copy(h, 1 - role).wait_send()
        own_copy(h, 1 - role).wait_send()
        for n in range(n_glob):
            @pl.when(is_far(n))
            def _(n=n):
                farpair_copy(h, n, role).wait_send()
                farone_copy(h, n, 1 - role).wait_send()
                farback_copy(h, n).wait_send()
        for j in range(1, bits):
            two_copy(h, j).wait_send()
        three_copy(h, role).wait_send()
        three_copy(h, 1 - role).wait_recv()
        for which, ref in enumerate((dkey_ref, dvalue_ref)):
            ref[pl.ds(h, tok, stride=heads), :] = wide(out_ref[which, h]).reshape(tok, dim)
        return carry

    lax.fori_loop(0, heads, finish, 0)


def write_kernel(*refs):
    sems = refs[8]
    copies = [pltpu.make_async_copy(refs[n], refs[4 + n], sems.at[n]) for n in range(4)]
    for c in copies:
        c.start()
    for c in copies:
        c.wait()


def shards(queries, key_states, value_states, out_grad, band_offsets, global_blocks):
    tok, heads, group, dim = queries.shape
    own = tok // BLK
    ctx_count, sections = lax.axis_size("ctx"), lax.axis_size("section")
    bits = sections.bit_length() - 1
    all_blocks = own * ctx_count
    stride_blocks = all_blocks // NGLOB
    n_glob = global_count(all_blocks, stride_blocks, own)
    slots = 2 * own + n_glob
    flat, narrow = (tok * heads * group, dim), (tok * heads, dim)
    hbm, vmem = pl.BlockSpec(memory_space=pltpu.HBM), pl.BlockSpec(memory_space=pltpu.VMEM)

    def low(*lead):
        return pltpu.VMEM((*lead, BLK, dim), jnp.bfloat16)

    def sems(*dims):
        return [pltpu.SemaphoreType.DMA(dims)] * 2

    att, dq, dkey, dvalue = pl.pallas_call(
        functools.partial(fused_kernel, own, n_glob, stride_blocks // own, ctx_count, bits, dim ** (-0.5), group),
        in_specs=[hbm] * 6,
        out_specs=[vmem] * 4,
        out_shape=[
            jax.ShapeDtypeStruct(flat, jnp.bfloat16),
            jax.ShapeDtypeStruct(flat, jnp.float32),
            jax.ShapeDtypeStruct(narrow, jnp.float32),
            jax.ShapeDtypeStruct(narrow, jnp.float32),
        ],
        scratch_shapes=[
            pltpu.SMEM(band_offsets.shape[::-1], jnp.int32), pltpu.SMEM(global_blocks.shape[::-1], jnp.int32),
            pltpu.VMEM(flat, jnp.bfloat16), pltpu.VMEM(flat, jnp.bfloat16), pltpu.VMEM((2, *narrow), jnp.bfloat16),
            pltpu.SemaphoreType.DMA((6,)),
            pltpu.VMEM(narrow, jnp.float32), low(2, heads, own),
            pltpu.VMEM(flat, jnp.float32), pltpu.VMEM(flat, jnp.float32), pltpu.VMEM(flat, jnp.float32),
            low(2, heads, own),
            low(2, heads, own + n_glob),
            pltpu.VMEM((2, slots, BLK, dim), jnp.float32),
            pltpu.VMEM((own, BLK, dim), jnp.float32),
            low(2, heads, slots), low(heads, slots), low(heads, slots), low(heads, own), low(heads, ctx_count),
            low(bits, heads, own), low(bits, heads, own),
            *sems(heads), pltpu.SemaphoreType.DMA((heads, ctx_count)), pltpu.SemaphoreType.DMA((heads, n_glob)),
            *sems(heads), *sems(heads, n_glob),
            *sems(heads), *sems(heads), *sems(heads, n_glob),
            *sems(heads), pltpu.SemaphoreType.DMA((heads, n_glob)), pltpu.SemaphoreType.DMA((heads, ctx_count)),
            *sems(bits, heads), *sems(heads),
        ],
        compiler_params=pltpu.CompilerParams(
            vmem_limit_bytes=40 * 2**20, collective_id=0, has_side_effects=True),
    )(*(pltpu.with_memory_space_constraint(x, pltpu.HBM) for x in (
        band_offsets.T, global_blocks.T, queries.reshape(flat), out_grad.reshape(flat),
        key_states.reshape(narrow), value_states.reshape(narrow))))
    results = (att, dq, dkey, dvalue)
    att, dq, dkey, dvalue = pl.pallas_call(
        write_kernel,
        in_specs=[vmem] * 4,
        out_specs=[hbm] * 4,
        out_shape=[jax.ShapeDtypeStruct(x.shape, x.dtype) for x in results],
        scratch_shapes=[pltpu.SemaphoreType.DMA((4,))],
        compiler_params=pltpu.CompilerParams(vmem_limit_bytes=2**20),
    )(*results)
    return (att.reshape(queries.shape), dq.reshape(queries.shape), dkey.reshape(key_states.shape),
            dvalue.reshape(key_states.shape))


def solution(mesh):
    wide, narrow = P("ctx", "tp", "section", None), P("ctx", "tp", None)
    return jax.shard_map(
        shards,
        mesh=mesh,
        in_specs=(wide, narrow, narrow, wide, P(), P()),
        out_specs=(wide, wide, narrow, narrow),
        check_vma=False,
    )
```

```python
import functools

import jax
import jax.numpy as jnp
from jax import lax
from jax.experimental import pallas as pl
from jax.experimental.pallas import tpu as pltpu
from jax.sharding import PartitionSpec as P

BLK = 128
NBAND = 3
NGLOB = 4
REACH = ((1, 2), (3, 4))
LOG2E = 1.4426950408889634
LOW = -1e30


def global_count(all_blocks, stride_blocks, own_blocks):
    return len([n for n in range(NGLOB) if n * stride_blocks < all_blocks - 1 - own_blocks])


def dot_nt(a, b):
    return lax.dot_general(a, b, (((1,), (1,)), ((), ())), preferred_element_type=jnp.float32)


def dot_tn(a, b):
    return lax.dot_general(a, b, (((0,), (0,)), ((), ())), preferred_element_type=jnp.float32)


def dot_nn(a, b):
    return lax.dot_general(a, b, (((1,), (0,)), ((), ())), preferred_element_type=jnp.float32)


def when(cond):
    if isinstance(cond, bool):
        return (lambda action: action()) if cond else (lambda action: None)
    return pl.when(cond)


def wide(x):
    return x.astype(jnp.float32)


def block_rows(scale, rows):
    state = [dict() for _ in rows]

    def scores(r, v):
        def selected(block_of):
            parts = [block_of(r["diag"])]
            for off, (reach, near, far) in zip(r["offs"], r["bands"]):
                parts.append(jnp.where(off == reach, block_of(near), block_of(far)))
            return jnp.concatenate(parts + [block_of(slot) for slot in r["globs"]], axis=0)

        v["q"] = r["q"]()
        v["keys"] = selected(r["key_of"])
        v["scores"] = dot_nt(v["keys"], v["q"])
        v["values"] = selected(r["value_of"])

    def softmax(r, v):
        scores = v["scores"]
        width = scores.shape[1]
        key_pos = lax.broadcasted_iota(jnp.int32, (BLK, width), 0)
        query_pos = lax.broadcasted_iota(jnp.int32, (BLK, width), 1) % BLK
        pieces = [jnp.where(key_pos <= query_pos, scores[:BLK], LOW)]
        pieces += [scores[n * BLK:(n + 1) * BLK] for n in range(1, len(r["oks"]) + 1)]
        bias = [jnp.float32(0.0)] + [jnp.where(ok, 0.0, LOW) for ok in r["oks"]]
        top = functools.reduce(jnp.maximum, [jnp.max(x, axis=0, keepdims=True) + b for x, b in zip(pieces, bias)])
        probs = jnp.concatenate(
            [jnp.exp2((x - (top - b)) * (scale * LOG2E)) for x, b in zip(pieces, bias)], axis=0)
        v["share"] = 1.0 / jnp.sum(probs, axis=0, keepdims=True)
        v["probs"], v["low"] = probs, probs.astype(jnp.bfloat16)

    def attend(r, v):
        att = wide((dot_tn(v["values"], v["low"]) * v["share"]).astype(jnp.bfloat16))
        r["put_att"](att.T)
        v["g"] = (wide(r["g"]()).T * v["share"]).astype(jnp.bfloat16)
        v["dots"] = jnp.sum(wide(v["g"]) * att, axis=0, keepdims=True)

    def score_grads(r, v):
        v["ds"] = (v["probs"] * (dot_nn(v["values"], v["g"]) - v["dots"])).astype(jnp.bfloat16)

    def grads(r, v):
        r["put_dq"]((dot_tn(v["keys"], v["ds"]) * scale).T)
        dk, dv = dot_nn(v["ds"], v["q"]) * scale, dot_nt(v["low"], v["g"])
        add = r["add"]
        for which, part in enumerate((dk, dv)):
            def piece(n):
                return part[n * BLK:(n + 1) * BLK]

            add(which, r["diag"], piece(0))
            for m, (off, (reach, near, far)) in enumerate(zip(r["offs"], r["bands"])):
                add(which, near, jnp.where(off == reach, piece(m + 1), 0.0))
                add(which, far, jnp.where(off == reach, 0.0, piece(m + 1)))
            for n, slot in enumerate(r["globs"]):
                add(which, slot, piece(NBAND + n))

    stages = (scores, softmax, attend, score_grads, grads)
    for t in range(len(stages) + len(rows) - 1):
        for n, row in enumerate(rows):
            if 0 <= t - n < len(stages):
                stages[t - n](row, state[n])


def fused_kernel(own, n_glob, owner_step, ctx_count, bits, scale, group, band_hbm, glob_hbm, q_hbm, g_hbm,
                 key_hbm, value_hbm, att_ref, dq_ref, dkey_ref, dvalue_ref,
                 band_ref, glob_ref, q_ref, g_ref, kv_in, load_s, kv_wide, seen, q_wide, g_wide, att_wide,
                 out_ref, acc, acc_own, parts, paired, halves, returned, farback, totals, swapped,
                 pieces, from_own, from_near, from_far, acc_share,
                 near_s, near_r, far_s, far_r, pair_s, pair_r, farpair_s, farpair_r,
                 one_s, one_r, own_s, own_r, farone_s, farone_r, back_s, back_r, farback_s, farback_r,
                 two_s, two_r, three_s, three_r,
                 piece_s, piece_r, nearpiece_s, nearpiece_r, farpiece_s, farpiece_r, spread_s, spread_r):
    sections, share = pieces.shape[0], pieces.shape[-2]
    heads, dim = seen.shape[1], seen.shape[-1]
    tok, lanes = own * BLK, heads * group
    mine = pl.ds(own, own)

    loads = [pltpu.make_async_copy(src, dst, load_s.at[n]) for n, (src, dst) in enumerate((
        (key_hbm, kv_in.at[0]), (value_hbm, kv_in.at[1]), (q_hbm, q_ref), (g_hbm, g_ref),
        (band_hbm, band_ref), (glob_hbm, glob_ref)))]
    for load in loads:
        load.start()
    p, s, parity = lax.axis_index("ctx"), lax.axis_index("section"), lax.axis_index("tp") % 2

    def other(j):
        bit = (1 << (j % bits)) * (1 - parity) + (1 << ((j + 1) % bits)) * parity
        side = (s // bit) % 2
        return s + bit * (1 - 2 * side), side

    mate, role = other(0)
    has_prev, has_next = p > 0, p < ctx_count - 1
    index = p // owner_step

    def owns(at):
        return jnp.logical_and(at % owner_step == 0, at // owner_step < n_glob)

    def sends_far(d):
        return jnp.logical_and(owns(p), p + d < ctx_count)

    def gets_far(d):
        return jnp.logical_and(p - d >= 0, owns(p - d + (p - d < 0) * ctx_count * owner_step))

    spans = range(2, ctx_count)

    def is_far(n):
        return p >= n * owner_step + 2

    def glob_slot(n):
        return jnp.where(p == n * owner_step + 1, 0, 2 * own + n)

    def copy(src, dst, ss, rs, axis, to):
        return pltpu.make_async_remote_copy(src_ref=src, dst_ref=dst, send_sem=ss, recv_sem=rs,
                                            device_id={axis: to}, device_id_type=pl.DeviceIdType.MESH)

    bar = pltpu.get_barrier_semaphore()
    def greet(ctx, section):
        pl.semaphore_signal(bar, inc=1, device_id={"ctx": ctx, "section": section},
                            device_id_type=pl.DeviceIdType.MESH)

    links = [(has_prev, p - 1), (has_next, p + 1)]
    for d in spans:
        links += [(sends_far(d), p + d), (gets_far(d), p - d)]
    for d in range(1, sections):
        greet(p, (s + d) % sections)
    for cond, to in links:
        @pl.when(cond)
        def _(to=to):
            for q in range(sections):
                greet(to, q)
    peers = sections - 1
    for cond, _ in links:
        peers = peers + jnp.where(cond, sections, 0)
    loads[0].wait()
    loads[1].wait()

    def split_heads(which):
        kv_wide[...] = wide(kv_in[which])
        for h in range(heads):
            seen[which, h, mine] = kv_wide[pl.ds(h, tok, stride=heads), :].astype(seen.dtype).reshape(own, BLK, dim)

    split_heads(0)
    split_heads(1)
    pl.semaphore_wait(bar, peers)

    def near_copy(h, b, n):
        return copy(seen.at[role, h, pl.ds(own + b, n)], seen.at[role, h, pl.ds(b, n)],
                    near_s.at[h, b], near_r.at[h, b], "ctx", p + 1)

    def rows_of(slot, h, section):
        return seen.at[:, h, slot, pl.ds(pl.multiple_of(section * share, share), share)]

    def far_copy(h, d):
        return copy(rows_of(own, h, s), rows_of(2 * own + index, h, s), far_s.at[h, d], far_r.at[h, index],
                    "ctx", p + d)

    def far_arrival(h, n):
        return copy(rows_of(own, h, s), rows_of(2 * own + n, h, s), far_s.at[h, 0], far_r.at[h, n], "ctx", p)

    def pair_copy(h, b, n, half):
        blocks = seen.at[half, h, pl.ds(b, n)]
        return copy(blocks, blocks, pair_s.at[h, b], pair_r.at[h, b], "section", mate)

    def farshare_copy(h, n, to, origin):
        rows = rows_of(2 * own + n, h, origin)
        return copy(rows, rows, farpair_s.at[h, n, to], farpair_r.at[h, n, origin], "section", to)

    def one_copy(h, src_half):
        return copy(parts.at[src_half, h, pl.ds(0, own)], paired.at[h, pl.ds(0, own)],
                    one_s.at[h], one_r.at[h], "section", mate)

    def own_copy(h, src_half):
        return copy(parts.at[src_half, h, mine], paired.at[h, mine], own_s.at[h], own_r.at[h], "section", mate)

    def farone_copy(h, n, src_half):
        return copy(parts.at[src_half, h, 2 * own + n], paired.at[h, 2 * own + n],
                    farone_s.at[h, n], farone_r.at[h, n], "section", mate)

    def back_copy(h):
        return copy(halves.at[h, pl.ds(0, own)], returned.at[h], back_s.at[h], back_r.at[h], "ctx", p - 1)

    def farback_copy(h, n):
        return copy(halves.at[h, own + n], farback.at[h, p - n * owner_step], farback_s.at[h, n],
                    farback_r.at[h, p - n * owner_step], "ctx", n * owner_step)

    def farback_arrival(h, d):
        return copy(halves.at[h, own], farback.at[h, d], farback_s.at[h, 0], farback_r.at[h, d], "ctx", p)

    def two_copy(h, j):
        return copy(totals.at[j, h], swapped.at[j, h], two_s.at[j, h], two_r.at[j, h], "section", other(j)[0])

    def three_copy(h, half):
        return copy(out_ref.at[half, h], out_ref.at[half, h], three_s.at[h], three_r.at[h], "section", mate)

    def piece_of(src, dst, ss, rs, ctx, section):
        return pltpu.make_async_remote_copy(src_ref=src, dst_ref=dst, send_sem=ss, recv_sem=rs,
                                            device_id={"ctx": ctx, "section": section},
                                            device_id_type=pl.DeviceIdType.MESH)

    def own_piece(to, origin):
        return piece_of(pieces.at[to, :, mine], from_own.at[origin], piece_s.at[to], piece_r.at[origin], p, to)

    early, late = pl.ds(0, own - 2), pl.ds(own - 2, 2)

    def near_piece(to, origin, n):
        at = (early, late)[n]
        return piece_of(pieces.at[to, :, at], from_near.at[origin, :, at], nearpiece_s.at[to, n],
                        nearpiece_r.at[origin, n], p - 1, to)

    def far_piece(to, origin, n, d):
        return piece_of(pieces.at[to, :, 2 * own + n], from_far.at[d, origin], farpiece_s.at[n, to],
                        farpiece_r.at[d, origin], n * owner_step, to)

    def share_of(n, section):
        at = (pl.ds(1, own - 1), pl.ds(0, 1))[n]
        return out_ref.at[:, heads - 1, at, pl.ds(pl.multiple_of(section * share, share), share)]

    def spread_copy(to, origin, n):
        return piece_of(share_of(n, origin), share_of(n, origin), spread_s.at[to, n], spread_r.at[origin, n], p, to)

    first = (0, own - 1)
    rest = tuple(range(own - 2, 0, -1))

    def groups(h):
        return [(b, 1) for b in first + rest] if isinstance(h, int) and h == 0 else [(0, own)]

    for h in range(heads):
        for d in spans:
            @pl.when(sends_far(d))
            def _(h=h, d=d):
                far_copy(h, d).start()

        @pl.when(has_next)
        def _(h=h):
            for b, n in groups(h):
                near_copy(h, b, n).start()

    @pl.when(jnp.logical_not(has_prev))
    def _():
        seen[:, :, :own] = jnp.zeros_like(seen[:, :, :own])
    for n in range(n_glob):
        @pl.when(p < n * owner_step + 1)
        def _(n=n):
            seen[:, :, 2 * own + n] = jnp.zeros_like(seen[:, :, 2 * own + n])

    def pass_far(h):
        for n in range(n_glob):
            @pl.when(is_far(n))
            def _(n=n):
                far_arrival(h, n).wait_recv()
                for d in range(1, sections):
                    farshare_copy(h, n, (s + d) % sections, s).start()

    def pass_near(h):
        @pl.when(has_prev)
        def _():
            for b, n in groups(h):
                near_copy(h, b, n).wait_recv()
                pair_copy(h, b, n, role).start()

    def arrived_far(h):
        for n in range(n_glob):
            @pl.when(is_far(n))
            def _(n=n):
                for d in range(1, sections):
                    farshare_copy(h, n, s, (s + d) % sections).wait_recv()

    def arrived_near(h, blocks):
        @pl.when(has_prev)
        def _():
            for b, n in blocks:
                pair_copy(h, b, n, 1 - role).wait_recv()

    def row_of(h, i):
        row = p * own + i
        spots = [pl.ds(i * (BLK * lanes) + h * group + n, BLK, stride=lanes) for n in range(group)]

        def rows_in(ref):
            return lambda: jnp.concatenate([ref[at, :] for at in spots], axis=0).astype(jnp.bfloat16)

        def put_in(ref):
            def put(x):
                for n, at in enumerate(spots):
                    ref[at, :] = x[n * BLK:(n + 1) * BLK]
            return put

        def block_of(which):
            return lambda slot: seen[which, h, slot]

        def add(which, slot, part):
            acc[which, slot] += part

        offs = [band_ref[1 + m, row] for m in range(NBAND - 1)]
        return dict(offs=offs, oks=[o >= 0 for o in offs] + [glob_ref[n, row] >= 0 for n in range(n_glob)],
                    bands=[(near, own + i - near, own + i - far) for near, far in REACH], diag=own + i,
                    globs=[glob_slot(n) for n in range(n_glob)], q=rows_in(q_wide), g=rows_in(g_wide),
                    key_of=block_of(0), value_of=block_of(1), put_att=put_in(att_wide), put_dq=put_in(dq_ref), add=add)

    def compute(h, rows):
        block_rows(scale, [row_of(h, i) for i in rows])

    def send_parts(h):
        parts[:, h] = acc[...].astype(parts.dtype)

        @pl.when(has_prev)
        def _():
            one_copy(h, 1 - role).start()
        for n in range(n_glob):
            @pl.when(is_far(n))
            def _(n=n):
                farone_copy(h, n, 1 - role).start()
        own_copy(h, 1 - role).start()

    def send_back(h):
        @pl.when(has_prev)
        def _():
            one_copy(h, role).wait_recv()
            near = pl.ds(0, own)
            halves[h, near] = (wide(parts[role, h, near]) + wide(paired[h, near])).astype(halves.dtype)
            back_copy(h).start()
        for n in range(n_glob):
            @pl.when(is_far(n))
            def _(n=n):
                farone_copy(h, n, role).wait_recv()
                at = 2 * own + n
                halves[h, own + n] = (wide(parts[role, h, at]) + wide(paired[h, at])).astype(halves.dtype)
                farback_copy(h, n).start()

    def swap(h):
        own_copy(h, role).wait_recv()
        acc_own[...] = wide(parts[role, h, mine]) + wide(paired[h, mine])

        @pl.when(has_next)
        def _():
            back_copy(h).wait_recv()
            acc_own[...] += wide(returned[h])
        for d in spans:
            @pl.when(sends_far(d))
            def _(d=d):
                farback_arrival(h, d).wait_recv()
                acc_own[0] += wide(farback[h, d])
        totals[1, h] = acc_own[...].astype(totals.dtype)
        two_copy(h, 1).start()

    def spread(h):
        for j in range(1, bits):
            two_copy(h, j).wait_recv()
            result = (wide(totals[j, h]) + wide(swapped[j, h])).astype(totals.dtype)
            if j + 1 < bits:
                totals[j + 1, h] = result
                two_copy(h, j + 1).start()
            else:
                out_ref[role, h] = result
        three_copy(h, role).start()

    def finish(h):
        three_copy(h, 1 - role).wait_recv()
        write_keys(h)

    def cut_piece(slot, at):
        for q in range(sections):
            pieces[q, :, at] = acc[:, slot, q * share:(q + 1) * share].astype(pieces.dtype)

    def send_near_pieces(n):
        for at in range(own)[:own - 2] if n == 0 else range(own)[own - 2:]:
            cut_piece((at + 1) % own, at)

        @pl.when(has_prev)
        def _():
            for d in range(sections):
                near_piece((s + d) % sections, s, n).start()

    def send_pieces():
        send_near_pieces(1)
        for b in range(own, 2 * own):
            cut_piece(b, b)
        for d in range(1, sections):
            own_piece((s + d) % sections, s).start()
        for n in range(n_glob):
            cut_piece(2 * own + n, 2 * own + n)

            @pl.when(is_far(n))
            def _(n=n):
                for d in range(sections):
                    far_piece((s + d) % sections, s, n, p - n * owner_step).start()

    def sum_pieces():
        rows = pl.ds(pl.multiple_of(s * share, share), share)
        total = wide(pieces[s, :, mine])
        for d in range(1, sections):
            origin = (s + d) % sections
            own_piece(s, origin).wait_recv()
            total += wide(from_own[origin])
        acc_share[...] = total

        @pl.when(has_next)
        def _():
            for q in range(sections):
                for n in range(2):
                    near_piece(s, q, n).wait_recv()
            for b in range(own):
                acc_share[:, b] += sum(wide(from_near[q, :, (b + own - 1) % own]) for q in range(sections))
        out_ref[:, heads - 1, 1:own, rows] = acc_share[:, 1:].astype(out_ref.dtype)
        for d in range(1, sections):
            spread_copy((s + d) % sections, s, 0).start()
        for d in spans:
            @pl.when(sends_far(d))
            def _(d=d):
                for q in range(sections):
                    far_piece(s, q, 0, d).wait_recv()
                acc_share[:, 0] += sum(wide(from_far[d, q]) for q in range(sections))
        out_ref[:, heads - 1, 0:1, rows] = acc_share[:, 0:1].astype(out_ref.dtype)
        for d in range(1, sections):
            spread_copy((s + d) % sections, s, 1).start()

    def write_keys(h):
        for which, ref in enumerate((dkey_ref, dvalue_ref)):
            ref[pl.ds(h, tok, stride=heads), :] = wide(out_ref[which, h]).reshape(tok, dim)

    for load in loads[2:]:
        load.wait()
    q_wide[...] = wide(q_ref[...])
    g_wide[...] = wide(g_ref[...])
    pass_far(0)
    pass_near(0)
    final = heads - 1

    def head(h):
        one_head = isinstance(h, int) and h == 0
        arrived_far(h)
        arrived_near(h, groups(h)[:2])
        acc[...] = jnp.zeros_like(acc)
        for k in range(own):
            if k > 0 and one_head:
                arrived_near(h, groups(h)[k + 1:k + 2])
            if k % 2 == 1:
                compute(h, [own - k, own - 1 - k] if one_head else [k - 1, k])
            if k == 0:
                @when(h >= 2)
                def _():
                    swap(h - 2)
            if k == 1:
                @when(h + 1 < heads)
                def _():
                    pass_far(h + 1)
                    pass_near(h + 1)

                @when(h >= 1)
                def _():
                    send_back(h - 1)
            if k == own - 1 and isinstance(h, int) and h == final:
                send_near_pieces(0)
            if k == own - 1:
                if isinstance(h, int) and h == final:
                    send_pieces()
                else:
                    send_parts(h)

                @when(h >= 2)
                def _():
                    spread(h - 2)

    head(0)

    def middle(h, carry):
        head(h)
        return carry

    lax.fori_loop(1, final, middle, 0)
    head(final)
    swap(final - 1)
    att_ref[...] = att_wide[...].astype(att_ref.dtype)
    for h in range(final - 1):
        finish(h)
    spread(final - 1)
    sum_pieces()
    finish(final - 1)
    for n in range(2):
        for d in range(1, sections):
            spread_copy(s, (s + d) % sections, n).wait_recv()
    write_keys(final)

    def drain(h):
        @pl.when(has_next)
        def _():
            for b, n in groups(h):
                near_copy(h, b, n).wait_send()
        for d in spans:
            @pl.when(sends_far(d))
            def _(d=d):
                far_copy(h, d).wait_send()

        @pl.when(has_prev)
        def _():
            for b, n in groups(h):
                pair_copy(h, b, n, role).wait_send()
        for n in range(n_glob):
            @pl.when(is_far(n))
            def _(n=n):
                for d in range(1, sections):
                    farshare_copy(h, n, (s + d) % sections, s).wait_send()
        if h < final:
            @pl.when(has_prev)
            def _():
                one_copy(h, 1 - role).wait_send()
                back_copy(h).wait_send()
            own_copy(h, 1 - role).wait_send()
            for n in range(n_glob):
                @pl.when(is_far(n))
                def _(n=n):
                    farone_copy(h, n, 1 - role).wait_send()
                    farback_copy(h, n).wait_send()
            for j in range(1, bits):
                two_copy(h, j).wait_send()
            three_copy(h, role).wait_send()

    for h in range(heads):
        drain(h)
    for d in range(sections):
        to = (s + d) % sections

        @pl.when(has_prev)
        def _(to=to):
            for n in range(2):
                near_piece(to, s, n).wait_send()
        for n in range(n_glob):
            @pl.when(is_far(n))
            def _(n=n, to=to):
                far_piece(to, s, n, 0).wait_send()
        if d > 0:
            own_piece(to, s).wait_send()
            for n in range(2):
                spread_copy(to, s, n).wait_send()


def write_kernel(*refs):
    sems = refs[8]
    copies = [pltpu.make_async_copy(refs[n], refs[4 + n], sems.at[n]) for n in range(4)]
    for c in copies:
        c.start()
    for c in copies:
        c.wait()


def shards(queries, key_states, value_states, out_grad, band_offsets, global_blocks):
    tok, heads, group, dim = queries.shape
    own = tok // BLK
    ctx_count, sections = lax.axis_size("ctx"), lax.axis_size("section")
    bits = sections.bit_length() - 1
    all_blocks = own * ctx_count
    stride_blocks = all_blocks // NGLOB
    n_glob = global_count(all_blocks, stride_blocks, own)
    slots = 2 * own + n_glob
    flat, narrow = (tok * heads * group, dim), (tok * heads, dim)
    hbm, vmem = pl.BlockSpec(memory_space=pltpu.HBM), pl.BlockSpec(memory_space=pltpu.VMEM)

    def low(*lead):
        return pltpu.VMEM((*lead, BLK, dim), jnp.bfloat16)

    def cut(*lead):
        return pltpu.VMEM((*lead, BLK // sections, dim), jnp.bfloat16)

    def full(*shape):
        return pltpu.VMEM(shape, jnp.float32)

    def sems(*dims):
        return [pltpu.SemaphoreType.DMA(dims)] * 2

    results = pl.pallas_call(
        functools.partial(fused_kernel, own, n_glob, stride_blocks // own, ctx_count, bits, dim ** (-0.5), group),
        in_specs=[hbm] * 6,
        out_specs=[vmem] * 4,
        out_shape=[
            jax.ShapeDtypeStruct(flat, jnp.bfloat16),
            jax.ShapeDtypeStruct(flat, jnp.float32),
            jax.ShapeDtypeStruct(narrow, jnp.float32),
            jax.ShapeDtypeStruct(narrow, jnp.float32),
        ],
        scratch_shapes=[
            pltpu.SMEM(band_offsets.shape[::-1], jnp.int32), pltpu.SMEM(global_blocks.shape[::-1], jnp.int32),
            pltpu.VMEM(flat, jnp.bfloat16), pltpu.VMEM(flat, jnp.bfloat16), pltpu.VMEM((2, *narrow), jnp.bfloat16),
            pltpu.SemaphoreType.DMA((6,)),
            full(*narrow), low(2, heads, slots), full(*flat), full(*flat), full(*flat),
            low(2, heads, own), full(2, slots, BLK, dim), full(own, BLK, dim),
            low(2, heads, slots), low(heads, slots), low(heads, own + n_glob), low(heads, own), low(heads, ctx_count),
            low(bits, heads, own), low(bits, heads, own),
            cut(sections, 2, slots), cut(sections, 2, own), cut(sections, 2, own), cut(ctx_count, sections, 2),
            full(2, own, BLK // sections, dim),
            *sems(heads, own), pltpu.SemaphoreType.DMA((heads, ctx_count)), pltpu.SemaphoreType.DMA((heads, n_glob)),
            *sems(heads, own), *sems(heads, n_glob, sections),
            *sems(heads), *sems(heads), *sems(heads, n_glob),
            *sems(heads), pltpu.SemaphoreType.DMA((heads, n_glob)), pltpu.SemaphoreType.DMA((heads, ctx_count)),
            *sems(bits, heads), *sems(heads),
            *sems(sections), *sems(sections, 2),
            pltpu.SemaphoreType.DMA((n_glob, sections)), pltpu.SemaphoreType.DMA((ctx_count, sections)),
            *sems(sections, 2),
        ],
        compiler_params=pltpu.CompilerParams(
            vmem_limit_bytes=40 * 2**20, collective_id=0, has_side_effects=True),
    )(*(pltpu.with_memory_space_constraint(x, pltpu.HBM) for x in (
        band_offsets.T, global_blocks.T, queries.reshape(flat), out_grad.reshape(flat),
        key_states.reshape(narrow), value_states.reshape(narrow))))
    att, dq, dkey, dvalue = pl.pallas_call(
        write_kernel,
        in_specs=[vmem] * 4,
        out_specs=[hbm] * 4,
        out_shape=[jax.ShapeDtypeStruct(x.shape, x.dtype) for x in results],
        scratch_shapes=[pltpu.SemaphoreType.DMA((4,))],
        compiler_params=pltpu.CompilerParams(vmem_limit_bytes=2**20),
    )(*results)
    return (att.reshape(queries.shape), dq.reshape(queries.shape), dkey.reshape(key_states.shape),
            dvalue.reshape(key_states.shape))


def solution(mesh):
    wide_spec, narrow_spec = P("ctx", "tp", "section", None), P("ctx", "tp", None)
    return jax.shard_map(
        shards,
        mesh=mesh,
        in_specs=(wide_spec, narrow_spec, narrow_spec, wide_spec, P(), P()),
        out_specs=(wide_spec, wide_spec, narrow_spec, narrow_spec),
        check_vma=False,
    )
```

```python
import functools

import jax
import jax.numpy as jnp
from jax import lax
from jax.experimental import pallas as pl
from jax.experimental.pallas import tpu as pltpu
from jax.sharding import PartitionSpec as P

BLK = 128
NBAND = 3
NGLOB = 4
REACH = ((1, 2), (3, 4))
LOG2E = 1.4426950408889634
LOW = -1e30


def global_count(all_blocks, stride_blocks, own_blocks):
    return len([n for n in range(NGLOB) if n * stride_blocks < all_blocks - 1 - own_blocks])


def dot_nt(a, b):
    return lax.dot_general(a, b, (((1,), (1,)), ((), ())), preferred_element_type=jnp.float32)


def dot_tn(a, b):
    return lax.dot_general(a, b, (((0,), (0,)), ((), ())), preferred_element_type=jnp.float32)


def dot_nn(a, b):
    return lax.dot_general(a, b, (((1,), (0,)), ((), ())), preferred_element_type=jnp.float32)


def when(cond):
    if isinstance(cond, bool):
        return (lambda action: action()) if cond else (lambda action: None)
    return pl.when(cond)


def wide(x):
    return x.astype(jnp.float32)


def block_rows(scale, rows):
    state = [dict() for _ in rows]

    def scores(r, v):
        def selected(block_of):
            parts = [block_of(r["diag"])]
            for off, (reach, near, far) in zip(r["offs"], r["bands"]):
                parts.append(jnp.where(off == reach, block_of(near), block_of(far)))
            return jnp.concatenate(parts + [block_of(slot) for slot in r["globs"]], axis=0)

        v["q"] = r["q"]()
        v["keys"] = selected(r["key_of"])
        v["scores"] = dot_nt(v["keys"], v["q"])
        v["values"] = selected(r["value_of"])

    def softmax(r, v):
        scores = v["scores"]
        width = scores.shape[1]
        key_pos = lax.broadcasted_iota(jnp.int32, (BLK, width), 0)
        query_pos = lax.broadcasted_iota(jnp.int32, (BLK, width), 1) % BLK
        pieces = [jnp.where(key_pos <= query_pos, scores[:BLK], LOW)]
        pieces += [scores[n * BLK:(n + 1) * BLK] for n in range(1, len(r["oks"]) + 1)]
        bias = [jnp.float32(0.0)] + [jnp.where(ok, 0.0, LOW) for ok in r["oks"]]
        top = functools.reduce(jnp.maximum, [jnp.max(x, axis=0, keepdims=True) + b for x, b in zip(pieces, bias)])
        probs = jnp.concatenate(
            [jnp.exp2((x - (top - b)) * (scale * LOG2E)) for x, b in zip(pieces, bias)], axis=0)
        v["share"] = 1.0 / jnp.sum(probs, axis=0, keepdims=True)
        v["probs"], v["low"] = probs, probs.astype(jnp.bfloat16)

    def attend(r, v):
        att = wide((dot_tn(v["values"], v["low"]) * v["share"]).astype(jnp.bfloat16))
        r["put_att"](att.T)
        v["g"] = (wide(r["g"]()).T * v["share"]).astype(jnp.bfloat16)
        v["dots"] = jnp.sum(wide(v["g"]) * att, axis=0, keepdims=True)

    def score_grads(r, v):
        v["ds"] = (v["probs"] * (dot_nn(v["values"], v["g"]) - v["dots"])).astype(jnp.bfloat16)

    def grads(r, v):
        r["put_dq"]((dot_tn(v["keys"], v["ds"]) * scale).T)
        dk, dv = dot_nn(v["ds"], v["q"]) * scale, dot_nt(v["low"], v["g"])
        add = r["add"]
        for which, part in enumerate((dk, dv)):
            def piece(n):
                return part[n * BLK:(n + 1) * BLK]

            add(which, r["diag"], piece(0))
            for m, (off, (reach, near, far)) in enumerate(zip(r["offs"], r["bands"])):
                add(which, near, jnp.where(off == reach, piece(m + 1), 0.0))
                add(which, far, jnp.where(off == reach, 0.0, piece(m + 1)))
            for n, slot in enumerate(r["globs"]):
                add(which, slot, piece(NBAND + n))

    stages = (scores, softmax, attend, score_grads, grads)
    for t in range(len(stages) + len(rows) - 1):
        for n, row in enumerate(rows):
            if 0 <= t - n < len(stages):
                stages[t - n](row, state[n])


def fused_kernel(own, n_glob, owner_step, ctx_count, bits, scale, group, band_hbm, glob_hbm, q_hbm, g_hbm,
                 key_hbm, value_hbm, att_ref, dq_ref, dkey_ref, dvalue_ref,
                 band_ref, glob_ref, q_ref, g_ref, kv_in, load_s, kv_wide, seen, q_wide, g_wide, att_wide,
                 out_ref, acc, acc_own, parts, paired, halves, returned, farback, totals, swapped,
                 pieces, from_own, from_near, from_far, far_sum, far_got, acc_share,
                 near_s, near_r, far_s, far_r, pair_s, pair_r, farpair_s, farpair_r,
                 one_s, one_r, own_s, own_r, farone_s, farone_r, back_s, back_r, farback_s, farback_r,
                 two_s, two_r, three_s, three_r,
                 piece_s, piece_r, nearpiece_s, nearpiece_r, farpiece_s, farpiece_r, farsum_s, farsum_r, spread_s, spread_r):
    sections, share = pieces.shape[0], pieces.shape[-2]
    heads, dim = seen.shape[1], seen.shape[-1]
    tok, lanes = own * BLK, heads * group
    mine = pl.ds(own, own)

    loads = [pltpu.make_async_copy(src, dst, load_s.at[n]) for n, (src, dst) in enumerate((
        (key_hbm, kv_in.at[0]), (value_hbm, kv_in.at[1]), (q_hbm, q_ref), (g_hbm, g_ref),
        (band_hbm, band_ref), (glob_hbm, glob_ref)))]
    for load in loads:
        load.start()
    p, s, parity = lax.axis_index("ctx"), lax.axis_index("section"), lax.axis_index("tp") % 2

    def other(j):
        bit = (1 << (j % bits)) * (1 - parity) + (1 << ((j + 1) % bits)) * parity
        side = (s // bit) % 2
        return s + bit * (1 - 2 * side), side

    mate, role = other(0)
    has_prev, has_next = p > 0, p < ctx_count - 1
    index = p // owner_step

    def owns(at):
        return jnp.logical_and(at % owner_step == 0, at // owner_step < n_glob)

    def sends_far(d):
        return jnp.logical_and(owns(p), p + d < ctx_count)

    def gets_far(d):
        return jnp.logical_and(p - d >= 0, owns(p - d + (p - d < 0) * ctx_count * owner_step))

    spans = range(2, ctx_count)

    def is_far(n):
        return p >= n * owner_step + 2

    def glob_slot(n):
        return jnp.where(p == n * owner_step + 1, 0, 2 * own + n)

    def copy(src, dst, ss, rs, axis, to):
        return pltpu.make_async_remote_copy(src_ref=src, dst_ref=dst, send_sem=ss, recv_sem=rs,
                                            device_id={axis: to}, device_id_type=pl.DeviceIdType.MESH)

    bar = pltpu.get_barrier_semaphore()
    def greet(ctx, section):
        pl.semaphore_signal(bar, inc=1, device_id={"ctx": ctx, "section": section},
                            device_id_type=pl.DeviceIdType.MESH)

    links = [(has_prev, p - 1), (has_next, p + 1)]
    for d in spans:
        links += [(sends_far(d), p + d), (gets_far(d), p - d)]
    for d in range(1, sections):
        greet(p, (s + d) % sections)
    for cond, to in links:
        @pl.when(cond)
        def _(to=to):
            for q in range(sections):
                greet(to, q)
    peers = sections - 1
    for cond, _ in links:
        peers = peers + jnp.where(cond, sections, 0)
    loads[0].wait()
    loads[1].wait()

    def split_heads(which):
        kv_wide[...] = wide(kv_in[which])
        for h in range(heads):
            seen[which, h, mine] = kv_wide[pl.ds(h, tok, stride=heads), :].astype(seen.dtype).reshape(own, BLK, dim)

    split_heads(0)
    split_heads(1)
    pl.semaphore_wait(bar, peers)

    def near_copy(h, b, n):
        return copy(seen.at[role, h, pl.ds(own + b, n)], seen.at[role, h, pl.ds(b, n)],
                    near_s.at[h, b], near_r.at[h, b], "ctx", p + 1)

    def rows_of(slot, h, section):
        return seen.at[:, h, slot, pl.ds(pl.multiple_of(section * share, share), share)]

    def far_copy(h, d):
        return copy(rows_of(own, h, s), rows_of(2 * own + index, h, s), far_s.at[h, d], far_r.at[h, index],
                    "ctx", p + d)

    def far_arrival(h, n):
        return copy(rows_of(own, h, s), rows_of(2 * own + n, h, s), far_s.at[h, 0], far_r.at[h, n], "ctx", p)

    def pair_copy(h, b, n, half):
        blocks = seen.at[half, h, pl.ds(b, n)]
        return copy(blocks, blocks, pair_s.at[h, b], pair_r.at[h, b], "section", mate)

    def farshare_copy(h, n, to, origin):
        rows = rows_of(2 * own + n, h, origin)
        return copy(rows, rows, farpair_s.at[h, n, to], farpair_r.at[h, n, origin], "section", to)

    def one_copy(h, src_half):
        return copy(parts.at[src_half, h, pl.ds(0, own)], paired.at[h, pl.ds(0, own)],
                    one_s.at[h], one_r.at[h], "section", mate)

    def own_copy(h, src_half):
        return copy(parts.at[src_half, h, mine], paired.at[h, mine], own_s.at[h], own_r.at[h], "section", mate)

    def farone_copy(h, n, src_half):
        return copy(parts.at[src_half, h, 2 * own + n], paired.at[h, 2 * own + n],
                    farone_s.at[h, n], farone_r.at[h, n], "section", mate)

    def back_copy(h):
        return copy(halves.at[h, pl.ds(0, own)], returned.at[h], back_s.at[h], back_r.at[h], "ctx", p - 1)

    def farback_copy(h, n):
        return copy(halves.at[h, own + n], farback.at[h, p - n * owner_step], farback_s.at[h, n],
                    farback_r.at[h, p - n * owner_step], "ctx", n * owner_step)

    def farback_arrival(h, d):
        return copy(halves.at[h, own], farback.at[h, d], farback_s.at[h, 0], farback_r.at[h, d], "ctx", p)

    def two_copy(h, j):
        return copy(totals.at[j, h], swapped.at[j, h], two_s.at[j, h], two_r.at[j, h], "section", other(j)[0])

    def three_copy(h, half):
        return copy(out_ref.at[half, h], out_ref.at[half, h], three_s.at[h], three_r.at[h], "section", mate)

    def piece_of(src, dst, ss, rs, ctx, section):
        return pltpu.make_async_remote_copy(src_ref=src, dst_ref=dst, send_sem=ss, recv_sem=rs,
                                            device_id={"ctx": ctx, "section": section},
                                            device_id_type=pl.DeviceIdType.MESH)

    def own_piece(to, origin):
        return piece_of(pieces.at[to, :, mine], from_own.at[origin], piece_s.at[to], piece_r.at[origin], p, to)

    early, late = pl.ds(0, 1), pl.ds(1, own - 1)

    def near_piece(to, origin, n):
        at = (early, late)[n]
        return piece_of(pieces.at[to, :, at], from_near.at[origin, :, at], nearpiece_s.at[to, n],
                        nearpiece_r.at[origin, n], p - 1, to)

    def far_piece(to, origin, n):
        return piece_of(pieces.at[to, :, 2 * own + n], from_far.at[n, origin], farpiece_s.at[n, to],
                        farpiece_r.at[n, origin], p, to)

    def farsum_copy(n, d):
        return copy(far_sum.at[n], far_got.at[d], farsum_s.at[n], farsum_r.at[d], "ctx", n * owner_step)

    def share_of(n, section):
        at = (pl.ds(1, own - 1), pl.ds(0, 1))[n]
        return out_ref.at[:, heads - 1, at, pl.ds(pl.multiple_of(section * share, share), share)]

    def spread_copy(to, origin, n):
        return piece_of(share_of(n, origin), share_of(n, origin), spread_s.at[to, n], spread_r.at[origin, n], p, to)

    first = (0, own - 1)
    rest = tuple(range(own - 2, 0, -1))

    def groups(h):
        return [(b, 1) for b in first + rest] if isinstance(h, int) and h == 0 else [(0, own)]

    for h in range(heads):
        for d in spans:
            @pl.when(sends_far(d))
            def _(h=h, d=d):
                far_copy(h, d).start()

        @pl.when(has_next)
        def _(h=h):
            for b, n in groups(h):
                near_copy(h, b, n).start()

    @pl.when(jnp.logical_not(has_prev))
    def _():
        seen[:, :, :own] = jnp.zeros_like(seen[:, :, :own])
    for n in range(n_glob):
        @pl.when(p < n * owner_step + 1)
        def _(n=n):
            seen[:, :, 2 * own + n] = jnp.zeros_like(seen[:, :, 2 * own + n])

    def pass_far(h):
        for n in range(n_glob):
            @pl.when(is_far(n))
            def _(n=n):
                far_arrival(h, n).wait_recv()
                for d in range(1, sections):
                    farshare_copy(h, n, (s + d) % sections, s).start()

    def pass_near(h):
        @pl.when(has_prev)
        def _():
            for b, n in groups(h):
                near_copy(h, b, n).wait_recv()
                pair_copy(h, b, n, role).start()

    def arrived_far(h):
        for n in range(n_glob):
            @pl.when(is_far(n))
            def _(n=n):
                for d in range(1, sections):
                    farshare_copy(h, n, s, (s + d) % sections).wait_recv()

    def arrived_near(h, blocks):
        @pl.when(has_prev)
        def _():
            for b, n in blocks:
                pair_copy(h, b, n, 1 - role).wait_recv()

    def row_of(h, i):
        row = p * own + i
        spots = [pl.ds(i * (BLK * lanes) + h * group + n, BLK, stride=lanes) for n in range(group)]

        def rows_in(ref):
            return lambda: jnp.concatenate([ref[at, :] for at in spots], axis=0).astype(jnp.bfloat16)

        def put_in(ref):
            def put(x):
                for n, at in enumerate(spots):
                    ref[at, :] = x[n * BLK:(n + 1) * BLK]
            return put

        def block_of(which):
            return lambda slot: seen[which, h, slot]

        def add(which, slot, part):
            acc[which, slot] += part

        offs = [band_ref[1 + m, row] for m in range(NBAND - 1)]
        return dict(offs=offs, oks=[o >= 0 for o in offs] + [glob_ref[n, row] >= 0 for n in range(n_glob)],
                    bands=[(near, own + i - near, own + i - far) for near, far in REACH], diag=own + i,
                    globs=[glob_slot(n) for n in range(n_glob)], q=rows_in(q_wide), g=rows_in(g_wide),
                    key_of=block_of(0), value_of=block_of(1), put_att=put_in(att_wide), put_dq=put_in(dq_ref), add=add)

    def compute(h, rows):
        block_rows(scale, [row_of(h, i) for i in rows])

    def send_parts(h):
        parts[:, h] = acc[...].astype(parts.dtype)

        @pl.when(has_prev)
        def _():
            one_copy(h, 1 - role).start()
        for n in range(n_glob):
            @pl.when(is_far(n))
            def _(n=n):
                farone_copy(h, n, 1 - role).start()
        own_copy(h, 1 - role).start()

    def send_back(h):
        @pl.when(has_prev)
        def _():
            one_copy(h, role).wait_recv()
            near = pl.ds(0, own)
            halves[h, near] = (wide(parts[role, h, near]) + wide(paired[h, near])).astype(halves.dtype)
            back_copy(h).start()
        for n in range(n_glob):
            @pl.when(is_far(n))
            def _(n=n):
                farone_copy(h, n, role).wait_recv()
                at = 2 * own + n
                halves[h, own + n] = (wide(parts[role, h, at]) + wide(paired[h, at])).astype(halves.dtype)
                farback_copy(h, n).start()

    def swap(h):
        own_copy(h, role).wait_recv()
        acc_own[...] = wide(parts[role, h, mine]) + wide(paired[h, mine])

        @pl.when(has_next)
        def _():
            back_copy(h).wait_recv()
            acc_own[...] += wide(returned[h])
        for d in spans:
            @pl.when(sends_far(d))
            def _(d=d):
                farback_arrival(h, d).wait_recv()
                acc_own[0] += wide(farback[h, d])
        totals[1, h] = acc_own[...].astype(totals.dtype)
        two_copy(h, 1).start()

    def spread(h):
        for j in range(1, bits):
            two_copy(h, j).wait_recv()
            result = (wide(totals[j, h]) + wide(swapped[j, h])).astype(totals.dtype)
            if j + 1 < bits:
                totals[j + 1, h] = result
                two_copy(h, j + 1).start()
            else:
                out_ref[role, h] = result
        three_copy(h, role).start()

    def finish(h):
        three_copy(h, 1 - role).wait_recv()
        write_keys(h)

    def cut_piece(slot, at):
        for q in range(sections):
            pieces[q, :, at] = acc[:, slot, q * share:(q + 1) * share].astype(pieces.dtype)

    def send_near_pieces(n):
        for at in range(own)[:1] if n == 0 else range(own)[1:]:
            cut_piece((at + 1) % own, at)

        @pl.when(has_prev)
        def _():
            for d in range(sections):
                near_piece((s + d) % sections, s, n).start()

    def send_pieces():
        send_near_pieces(1)
        for b in range(own, 2 * own):
            cut_piece(b, b)
        for d in range(1, sections):
            own_piece((s + d) % sections, s).start()
        for n in range(n_glob):
            cut_piece(2 * own + n, 2 * own + n)

            @pl.when(is_far(n))
            def _(n=n):
                for d in range(1, sections):
                    far_piece((s + d) % sections, s, n).start()

    def send_far_sums():
        for n in range(n_glob):
            @pl.when(is_far(n))
            def _(n=n):
                total = wide(pieces[s, :, 2 * own + n])
                for d in range(1, sections):
                    origin = (s + d) % sections
                    far_piece(s, origin, n).wait_recv()
                    total += wide(from_far[n, origin])
                far_sum[n] = total.astype(far_sum.dtype)
                farsum_copy(n, p - n * owner_step).start()

    def sum_pieces():
        rows = pl.ds(pl.multiple_of(s * share, share), share)
        total = wide(pieces[s, :, mine])
        for d in range(1, sections):
            origin = (s + d) % sections
            own_piece(s, origin).wait_recv()
            total += wide(from_own[origin])
        acc_share[...] = total

        @pl.when(has_next)
        def _():
            for q in range(sections):
                for n in range(2):
                    near_piece(s, q, n).wait_recv()
            for b in range(own):
                acc_share[:, b] += sum(wide(from_near[q, :, (b + own - 1) % own]) for q in range(sections))
        out_ref[:, heads - 1, 1:own, rows] = acc_share[:, 1:].astype(out_ref.dtype)
        for d in range(1, sections):
            spread_copy((s + d) % sections, s, 0).start()
        for d in spans:
            @pl.when(sends_far(d))
            def _(d=d):
                farsum_copy(0, d).wait_recv()
                acc_share[:, 0] += wide(far_got[d])
        out_ref[:, heads - 1, 0:1, rows] = acc_share[:, 0:1].astype(out_ref.dtype)
        for d in range(1, sections):
            spread_copy((s + d) % sections, s, 1).start()

    def write_keys(h):
        for which, ref in enumerate((dkey_ref, dvalue_ref)):
            ref[pl.ds(h, tok, stride=heads), :] = wide(out_ref[which, h]).reshape(tok, dim)

    for load in loads[2:]:
        load.wait()
    q_wide[...] = wide(q_ref[...])
    g_wide[...] = wide(g_ref[...])
    pass_far(0)
    pass_near(0)
    final = heads - 1

    def head(h):
        one_head = isinstance(h, int) and h == 0
        arrived_far(h)
        arrived_near(h, groups(h)[:2])
        acc[...] = jnp.zeros_like(acc)
        for k in range(own):
            if k > 0 and one_head:
                arrived_near(h, groups(h)[k + 1:k + 2])
            if k % 2 == 1:
                compute(h, [own - k, own - 1 - k] if one_head else [k - 1, k])
            if k == 0:
                @when(h >= 2)
                def _():
                    swap(h - 2)
            if k == 1:
                @when(h + 1 < heads)
                def _():
                    pass_far(h + 1)
                    pass_near(h + 1)

                @when(h >= 1)
                def _():
                    send_back(h - 1)
            if k == 1 and isinstance(h, int) and h == final:
                send_near_pieces(0)
            if k == own - 1:
                if isinstance(h, int) and h == final:
                    send_pieces()
                else:
                    send_parts(h)

                @when(h >= 2)
                def _():
                    spread(h - 2)

    head(0)

    def middle(h, carry):
        head(h)
        return carry

    lax.fori_loop(1, final, middle, 0)
    head(final)
    swap(final - 1)
    send_far_sums()
    att_ref[...] = att_wide[...].astype(att_ref.dtype)
    for h in range(final - 1):
        finish(h)
    spread(final - 1)
    sum_pieces()
    finish(final - 1)
    for n in range(2):
        for d in range(1, sections):
            spread_copy(s, (s + d) % sections, n).wait_recv()
    write_keys(final)

    def drain(h):
        @pl.when(has_next)
        def _():
            for b, n in groups(h):
                near_copy(h, b, n).wait_send()
        for d in spans:
            @pl.when(sends_far(d))
            def _(d=d):
                far_copy(h, d).wait_send()

        @pl.when(has_prev)
        def _():
            for b, n in groups(h):
                pair_copy(h, b, n, role).wait_send()
        for n in range(n_glob):
            @pl.when(is_far(n))
            def _(n=n):
                for d in range(1, sections):
                    farshare_copy(h, n, (s + d) % sections, s).wait_send()
        if h < final:
            @pl.when(has_prev)
            def _():
                one_copy(h, 1 - role).wait_send()
                back_copy(h).wait_send()
            own_copy(h, 1 - role).wait_send()
            for n in range(n_glob):
                @pl.when(is_far(n))
                def _(n=n):
                    farone_copy(h, n, 1 - role).wait_send()
                    farback_copy(h, n).wait_send()
            for j in range(1, bits):
                two_copy(h, j).wait_send()
            three_copy(h, role).wait_send()

    for h in range(heads):
        drain(h)
    for d in range(sections):
        to = (s + d) % sections

        @pl.when(has_prev)
        def _(to=to):
            for n in range(2):
                near_piece(to, s, n).wait_send()
        for n in range(n_glob):
            @pl.when(is_far(n))
            def _(n=n, to=to, d=d):
                if d > 0:
                    far_piece(to, s, n).wait_send()
                else:
                    farsum_copy(n, p - n * owner_step).wait_send()
        if d > 0:
            own_piece(to, s).wait_send()
            for n in range(2):
                spread_copy(to, s, n).wait_send()


def write_kernel(*refs):
    sems = refs[8]
    copies = [pltpu.make_async_copy(refs[n], refs[4 + n], sems.at[n]) for n in range(4)]
    for c in copies:
        c.start()
    for c in copies:
        c.wait()


def shards(queries, key_states, value_states, out_grad, band_offsets, global_blocks):
    tok, heads, group, dim = queries.shape
    own = tok // BLK
    ctx_count, sections = lax.axis_size("ctx"), lax.axis_size("section")
    bits = sections.bit_length() - 1
    all_blocks = own * ctx_count
    stride_blocks = all_blocks // NGLOB
    n_glob = global_count(all_blocks, stride_blocks, own)
    slots = 2 * own + n_glob
    flat, narrow = (tok * heads * group, dim), (tok * heads, dim)
    hbm, vmem = pl.BlockSpec(memory_space=pltpu.HBM), pl.BlockSpec(memory_space=pltpu.VMEM)

    def low(*lead):
        return pltpu.VMEM((*lead, BLK, dim), jnp.bfloat16)

    def cut(*lead):
        return pltpu.VMEM((*lead, BLK // sections, dim), jnp.bfloat16)

    def full(*shape):
        return pltpu.VMEM(shape, jnp.float32)

    def sems(*dims):
        return [pltpu.SemaphoreType.DMA(dims)] * 2

    results = pl.pallas_call(
        functools.partial(fused_kernel, own, n_glob, stride_blocks // own, ctx_count, bits, dim ** (-0.5), group),
        in_specs=[hbm] * 6,
        out_specs=[vmem] * 4,
        out_shape=[
            jax.ShapeDtypeStruct(flat, jnp.bfloat16),
            jax.ShapeDtypeStruct(flat, jnp.float32),
            jax.ShapeDtypeStruct(narrow, jnp.float32),
            jax.ShapeDtypeStruct(narrow, jnp.float32),
        ],
        scratch_shapes=[
            pltpu.SMEM(band_offsets.shape[::-1], jnp.int32), pltpu.SMEM(global_blocks.shape[::-1], jnp.int32),
            pltpu.VMEM(flat, jnp.bfloat16), pltpu.VMEM(flat, jnp.bfloat16), pltpu.VMEM((2, *narrow), jnp.bfloat16),
            pltpu.SemaphoreType.DMA((6,)),
            full(*narrow), low(2, heads, slots), full(*flat), full(*flat), full(*flat),
            low(2, heads, own), full(2, slots, BLK, dim), full(own, BLK, dim),
            low(2, heads, slots), low(heads, slots), low(heads, own + n_glob), low(heads, own), low(heads, ctx_count),
            low(bits, heads, own), low(bits, heads, own),
            cut(sections, 2, slots), cut(sections, 2, own), cut(sections, 2, own), cut(n_glob, sections, 2),
            cut(n_glob, 2), cut(ctx_count, 2),
            full(2, own, BLK // sections, dim),
            *sems(heads, own), pltpu.SemaphoreType.DMA((heads, ctx_count)), pltpu.SemaphoreType.DMA((heads, n_glob)),
            *sems(heads, own), *sems(heads, n_glob, sections),
            *sems(heads), *sems(heads), *sems(heads, n_glob),
            *sems(heads), pltpu.SemaphoreType.DMA((heads, n_glob)), pltpu.SemaphoreType.DMA((heads, ctx_count)),
            *sems(bits, heads), *sems(heads),
            *sems(sections), *sems(sections, 2),
            *sems(n_glob, sections), pltpu.SemaphoreType.DMA((n_glob,)), pltpu.SemaphoreType.DMA((ctx_count,)),
            *sems(sections, 2),
        ],
        compiler_params=pltpu.CompilerParams(
            vmem_limit_bytes=40 * 2**20, collective_id=0, has_side_effects=True),
    )(*(pltpu.with_memory_space_constraint(x, pltpu.HBM) for x in (
        band_offsets.T, global_blocks.T, queries.reshape(flat), out_grad.reshape(flat),
        key_states.reshape(narrow), value_states.reshape(narrow))))
    att, dq, dkey, dvalue = pl.pallas_call(
        write_kernel,
        in_specs=[vmem] * 4,
        out_specs=[hbm] * 4,
        out_shape=[jax.ShapeDtypeStruct(x.shape, x.dtype) for x in results],
        scratch_shapes=[pltpu.SemaphoreType.DMA((4,))],
        compiler_params=pltpu.CompilerParams(vmem_limit_bytes=2**20),
    )(*results)
    return (att.reshape(queries.shape), dq.reshape(queries.shape), dkey.reshape(key_states.shape),
            dvalue.reshape(key_states.shape))


def solution(mesh):
    wide_spec, narrow_spec = P("ctx", "tp", "section", None), P("ctx", "tp", None)
    return jax.shard_map(
        shards,
        mesh=mesh,
        in_specs=(wide_spec, narrow_spec, narrow_spec, wide_spec, P(), P()),
        out_specs=(wide_spec, wide_spec, narrow_spec, narrow_spec),
        check_vma=False,
    )
```

```python
import functools

import jax
import jax.numpy as jnp
from jax import lax
from jax.experimental import pallas as pl
from jax.experimental.pallas import tpu as pltpu
from jax.sharding import PartitionSpec as P

BLK = 128
NBAND = 3
NGLOB = 4
REACH = ((1, 2), (3, 4))
LOG2E = 1.4426950408889634
LOW = -1e30


def global_count(all_blocks, stride_blocks, own_blocks):
    return len([n for n in range(NGLOB) if n * stride_blocks < all_blocks - 1 - own_blocks])


def dot_nt(a, b):
    return lax.dot_general(a, b, (((1,), (1,)), ((), ())), preferred_element_type=jnp.float32)


def dot_tn(a, b):
    return lax.dot_general(a, b, (((0,), (0,)), ((), ())), preferred_element_type=jnp.float32)


def dot_nn(a, b):
    return lax.dot_general(a, b, (((1,), (0,)), ((), ())), preferred_element_type=jnp.float32)


def when(cond):
    if isinstance(cond, bool):
        return (lambda action: action()) if cond else (lambda action: None)
    return pl.when(cond)


def wide(x):
    return x.astype(jnp.float32)


def block_rows(scale, rows):
    state = [dict() for _ in rows]

    def scores(r, v):
        def selected(block_of):
            parts = [block_of(r["diag"])]
            for off, (reach, near, far) in zip(r["offs"], r["bands"]):
                parts.append(jnp.where(off == reach, block_of(near), block_of(far)))
            return jnp.concatenate(parts + [block_of(slot) for slot in r["globs"]], axis=0)

        v["q"] = r["q"]()
        v["keys"] = selected(r["key_of"])
        v["scores"] = dot_nt(v["keys"], v["q"])
        v["values"] = selected(r["value_of"])

    def softmax(r, v):
        scores = v["scores"]
        width = scores.shape[1]
        key_pos = lax.broadcasted_iota(jnp.int32, (BLK, width), 0)
        query_pos = lax.broadcasted_iota(jnp.int32, (BLK, width), 1) % BLK
        pieces = [jnp.where(key_pos <= query_pos, scores[:BLK], LOW)]
        pieces += [scores[n * BLK:(n + 1) * BLK] for n in range(1, len(r["oks"]) + 1)]
        bias = [jnp.float32(0.0)] + [jnp.where(ok, 0.0, LOW) for ok in r["oks"]]
        top = functools.reduce(jnp.maximum, [jnp.max(x, axis=0, keepdims=True) + b for x, b in zip(pieces, bias)])
        probs = jnp.concatenate(
            [jnp.exp2((x - (top - b)) * (scale * LOG2E)) for x, b in zip(pieces, bias)], axis=0)
        v["share"] = 1.0 / jnp.sum(probs, axis=0, keepdims=True)
        v["probs"], v["low"] = probs, probs.astype(jnp.bfloat16)

    def attend(r, v):
        att = wide((dot_tn(v["values"], v["low"]) * v["share"]).astype(jnp.bfloat16))
        r["put_att"](att.T)
        v["g"] = (wide(r["g"]()).T * v["share"]).astype(jnp.bfloat16)
        v["dots"] = jnp.sum(wide(v["g"]) * att, axis=0, keepdims=True)

    def score_grads(r, v):
        v["ds"] = (v["probs"] * (dot_nn(v["values"], v["g"]) - v["dots"])).astype(jnp.bfloat16)

    def grads(r, v):
        r["put_dq"]((dot_tn(v["keys"], v["ds"]) * scale).T)
        dk, dv = dot_nn(v["ds"], v["q"]) * scale, dot_nt(v["low"], v["g"])
        add = r["add"]
        for which, part in enumerate((dk, dv)):
            def piece(n):
                return part[n * BLK:(n + 1) * BLK]

            add(which, r["diag"], piece(0))
            for m, (off, (reach, near, far)) in enumerate(zip(r["offs"], r["bands"])):
                add(which, near, jnp.where(off == reach, piece(m + 1), 0.0))
                add(which, far, jnp.where(off == reach, 0.0, piece(m + 1)))
            for n, slot in enumerate(r["globs"]):
                add(which, slot, piece(NBAND + n))

    stages = (scores, softmax, attend, score_grads, grads)
    for t in range(len(stages) + len(rows) - 1):
        for n, row in enumerate(rows):
            if 0 <= t - n < len(stages):
                stages[t - n](row, state[n])


def fused_kernel(own, n_glob, owner_step, ctx_count, bits, scale, group, band_hbm, glob_hbm, q_hbm, g_hbm,
                 key_hbm, value_hbm, att_ref, dq_ref, dkey_ref, dvalue_ref,
                 band_ref, glob_ref, q_ref, g_ref, kv_in, load_s, kv_wide, seen, q_wide, g_wide, att_wide,
                 out_ref, acc, acc_own, parts, paired, halves, returned, farback, totals, swapped,
                 pieces, from_own, from_near, from_far, far_sum, far_got, acc_share,
                 near_s, near_r, far_s, far_r, pair_s, pair_r, farpair_s, farpair_r,
                 one_s, one_r, own_s, own_r, farone_s, farone_r, back_s, back_r, farback_s, farback_r,
                 two_s, two_r, three_s, three_r,
                 piece_s, piece_r, nearpiece_s, nearpiece_r, farpiece_s, farpiece_r, farsum_s, farsum_r, spread_s, spread_r):
    sections, share = pieces.shape[0], pieces.shape[-2]
    heads, dim = seen.shape[1], seen.shape[-1]
    tok, lanes = own * BLK, heads * group
    mine = pl.ds(own, own)

    loads = [pltpu.make_async_copy(src, dst, load_s.at[n]) for n, (src, dst) in enumerate((
        (key_hbm, kv_in.at[0]), (value_hbm, kv_in.at[1]), (q_hbm, q_ref), (g_hbm, g_ref),
        (band_hbm, band_ref), (glob_hbm, glob_ref)))]
    for load in loads:
        load.start()
    p, s, parity = lax.axis_index("ctx"), lax.axis_index("section"), lax.axis_index("tp") % 2

    def other(j):
        bit = (1 << (j % bits)) * (1 - parity) + (1 << ((j + 1) % bits)) * parity
        side = (s // bit) % 2
        return s + bit * (1 - 2 * side), side

    mate, role = other(0)
    has_prev, has_next = p > 0, p < ctx_count - 1
    index = p // owner_step

    def owns(at):
        return jnp.logical_and(at % owner_step == 0, at // owner_step < n_glob)

    def sends_far(d):
        return jnp.logical_and(owns(p), p + d < ctx_count)

    def gets_far(d):
        return jnp.logical_and(p - d >= 0, owns(p - d + (p - d < 0) * ctx_count * owner_step))

    spans = range(2, ctx_count)

    def is_far(n):
        return p >= n * owner_step + 2

    def glob_slot(n):
        return jnp.where(p == n * owner_step + 1, 0, 2 * own + n)

    def copy(src, dst, ss, rs, axis, to):
        return pltpu.make_async_remote_copy(src_ref=src, dst_ref=dst, send_sem=ss, recv_sem=rs,
                                            device_id={axis: to}, device_id_type=pl.DeviceIdType.MESH)

    bar = pltpu.get_barrier_semaphore()
    def greet(ctx, section):
        pl.semaphore_signal(bar, inc=1, device_id={"ctx": ctx, "section": section},
                            device_id_type=pl.DeviceIdType.MESH)

    links = [(has_prev, p - 1), (has_next, p + 1)]
    for d in spans:
        links += [(sends_far(d), p + d), (gets_far(d), p - d)]
    for d in range(1, sections):
        greet(p, (s + d) % sections)
    for cond, to in links:
        @pl.when(cond)
        def _(to=to):
            for q in range(sections):
                greet(to, q)
    peers = sections - 1
    for cond, _ in links:
        peers = peers + jnp.where(cond, sections, 0)
    loads[0].wait()
    loads[1].wait()

    def split_heads(which):
        kv_wide[...] = wide(kv_in[which])
        for h in range(heads):
            seen[which, h, mine] = kv_wide[pl.ds(h, tok, stride=heads), :].astype(seen.dtype).reshape(own, BLK, dim)

    split_heads(0)
    split_heads(1)
    pl.semaphore_wait(bar, peers)

    def near_copy(h, b, n):
        return copy(seen.at[role, h, pl.ds(own + b, n)], seen.at[role, h, pl.ds(b, n)],
                    near_s.at[h, b], near_r.at[h, b], "ctx", p + 1)

    def rows_of(slot, h, section):
        return seen.at[:, h, slot, pl.ds(pl.multiple_of(section * share, share), share)]

    def far_copy(h, d):
        return copy(rows_of(own, h, s), rows_of(2 * own + index, h, s), far_s.at[h, d], far_r.at[h, index],
                    "ctx", p + d)

    def far_arrival(h, n):
        return copy(rows_of(own, h, s), rows_of(2 * own + n, h, s), far_s.at[h, 0], far_r.at[h, n], "ctx", p)

    def pair_copy(h, b, n, half):
        blocks = seen.at[half, h, pl.ds(b, n)]
        return copy(blocks, blocks, pair_s.at[h, b], pair_r.at[h, b], "section", mate)

    def farshare_copy(h, n, to, origin):
        rows = rows_of(2 * own + n, h, origin)
        return copy(rows, rows, farpair_s.at[h, n, to], farpair_r.at[h, n, origin], "section", to)

    def one_copy(h, src_half):
        return copy(parts.at[src_half, h, pl.ds(0, own)], paired.at[h, pl.ds(0, own)],
                    one_s.at[h], one_r.at[h], "section", mate)

    def own_copy(h, src_half):
        return copy(parts.at[src_half, h, mine], paired.at[h, mine], own_s.at[h], own_r.at[h], "section", mate)

    def farone_copy(h, n, src_half):
        return copy(parts.at[src_half, h, 2 * own + n], paired.at[h, 2 * own + n],
                    farone_s.at[h, n], farone_r.at[h, n], "section", mate)

    def back_copy(h):
        return copy(halves.at[h, pl.ds(0, own)], returned.at[h], back_s.at[h], back_r.at[h], "ctx", p - 1)

    def farback_copy(h, n):
        return copy(halves.at[h, own + n], farback.at[h, p - n * owner_step], farback_s.at[h, n],
                    farback_r.at[h, p - n * owner_step], "ctx", n * owner_step)

    def farback_arrival(h, d):
        return copy(halves.at[h, own], farback.at[h, d], farback_s.at[h, 0], farback_r.at[h, d], "ctx", p)

    def two_copy(h, j):
        return copy(totals.at[j, h], swapped.at[j, h], two_s.at[j, h], two_r.at[j, h], "section", other(j)[0])

    def three_copy(h, half):
        return copy(out_ref.at[half, h], out_ref.at[half, h], three_s.at[h], three_r.at[h], "section", mate)

    def piece_of(src, dst, ss, rs, ctx, section):
        return pltpu.make_async_remote_copy(src_ref=src, dst_ref=dst, send_sem=ss, recv_sem=rs,
                                            device_id={"ctx": ctx, "section": section},
                                            device_id_type=pl.DeviceIdType.MESH)

    def own_piece(to, origin):
        return piece_of(pieces.at[to, :, mine], from_own.at[origin], piece_s.at[to], piece_r.at[origin], p, to)

    early, late = pl.ds(0, 1), pl.ds(1, own - 1)

    def near_piece(to, origin, n):
        at = (early, late)[n]
        return piece_of(pieces.at[to, :, at], from_near.at[origin, :, at], nearpiece_s.at[to, n],
                        nearpiece_r.at[origin, n], p - 1, to)

    def far_piece(to, origin, n):
        return piece_of(pieces.at[to, :, 2 * own + n], from_far.at[n, origin], farpiece_s.at[n, to],
                        farpiece_r.at[n, origin], p, to)

    def farsum_copy(n, d):
        return copy(far_sum.at[n], far_got.at[d], farsum_s.at[n], farsum_r.at[d], "ctx", n * owner_step)

    def share_of(n, section):
        at = (pl.ds(1, own - 1), pl.ds(0, 1))[n]
        return out_ref.at[:, heads - 1, at, pl.ds(pl.multiple_of(section * share, share), share)]

    def spread_copy(to, origin, n):
        return piece_of(share_of(n, origin), share_of(n, origin), spread_s.at[to, n], spread_r.at[origin, n], p, to)

    first = (0, own - 1)
    rest = tuple(range(own - 2, 0, -1))

    def groups(h):
        return [(b, 1) for b in first + rest] if isinstance(h, int) and h == 0 else [(0, own)]

    for h in range(heads):
        for d in spans:
            @pl.when(sends_far(d))
            def _(h=h, d=d):
                far_copy(h, d).start()

        @pl.when(has_next)
        def _(h=h):
            for b, n in groups(h):
                near_copy(h, b, n).start()

    @pl.when(jnp.logical_not(has_prev))
    def _():
        seen[:, :, :own] = jnp.zeros_like(seen[:, :, :own])
    for n in range(n_glob):
        @pl.when(p < n * owner_step + 1)
        def _(n=n):
            seen[:, :, 2 * own + n] = jnp.zeros_like(seen[:, :, 2 * own + n])

    def pass_far(h):
        for n in range(n_glob):
            @pl.when(is_far(n))
            def _(n=n):
                far_arrival(h, n).wait_recv()
                for d in range(1, sections):
                    farshare_copy(h, n, (s + d) % sections, s).start()

    def pass_near(h):
        @pl.when(has_prev)
        def _():
            for b, n in groups(h):
                near_copy(h, b, n).wait_recv()
                pair_copy(h, b, n, role).start()

    def arrived_far(h):
        for n in range(n_glob):
            @pl.when(is_far(n))
            def _(n=n):
                for d in range(1, sections):
                    farshare_copy(h, n, s, (s + d) % sections).wait_recv()

    def arrived_near(h, blocks):
        @pl.when(has_prev)
        def _():
            for b, n in blocks:
                pair_copy(h, b, n, 1 - role).wait_recv()

    def row_of(h, i):
        row = p * own + i
        spots = [pl.ds(i * (BLK * lanes) + h * group + n, BLK, stride=lanes) for n in range(group)]

        def rows_in(ref):
            return lambda: jnp.concatenate([ref[at, :] for at in spots], axis=0).astype(jnp.bfloat16)

        def put_in(ref):
            def put(x):
                for n, at in enumerate(spots):
                    ref[at, :] = x[n * BLK:(n + 1) * BLK]
            return put

        def block_of(which):
            return lambda slot: seen[which, h, slot]

        def add(which, slot, part):
            acc[which, slot] += part

        offs = [band_ref[1 + m, row] for m in range(NBAND - 1)]
        return dict(offs=offs, oks=[o >= 0 for o in offs] + [glob_ref[n, row] >= 0 for n in range(n_glob)],
                    bands=[(near, own + i - near, own + i - far) for near, far in REACH], diag=own + i,
                    globs=[glob_slot(n) for n in range(n_glob)], q=rows_in(q_wide), g=rows_in(g_wide),
                    key_of=block_of(0), value_of=block_of(1), put_att=put_in(att_wide), put_dq=put_in(dq_ref), add=add)

    def compute(h, rows):
        block_rows(scale, [row_of(h, i) for i in rows])

    def send_parts(h):
        parts[:, h] = acc[...].astype(parts.dtype)

        @pl.when(has_prev)
        def _():
            one_copy(h, 1 - role).start()
        for n in range(n_glob):
            @pl.when(is_far(n))
            def _(n=n):
                farone_copy(h, n, 1 - role).start()
        own_copy(h, 1 - role).start()

    def send_back(h):
        @pl.when(has_prev)
        def _():
            one_copy(h, role).wait_recv()
            near = pl.ds(0, own)
            halves[h, near] = (wide(parts[role, h, near]) + wide(paired[h, near])).astype(halves.dtype)
            back_copy(h).start()
        for n in range(n_glob):
            @pl.when(is_far(n))
            def _(n=n):
                farone_copy(h, n, role).wait_recv()
                at = 2 * own + n
                halves[h, own + n] = (wide(parts[role, h, at]) + wide(paired[h, at])).astype(halves.dtype)
                farback_copy(h, n).start()

    def swap(h):
        own_copy(h, role).wait_recv()
        acc_own[...] = wide(parts[role, h, mine]) + wide(paired[h, mine])

        @pl.when(has_next)
        def _():
            back_copy(h).wait_recv()
            acc_own[...] += wide(returned[h])
        for d in spans:
            @pl.when(sends_far(d))
            def _(d=d):
                farback_arrival(h, d).wait_recv()
                acc_own[0] += wide(farback[h, d])
        totals[1, h] = acc_own[...].astype(totals.dtype)
        two_copy(h, 1).start()

    def spread(h):
        for j in range(1, bits):
            two_copy(h, j).wait_recv()
            result = (wide(totals[j, h]) + wide(swapped[j, h])).astype(totals.dtype)
            if j + 1 < bits:
                totals[j + 1, h] = result
                two_copy(h, j + 1).start()
            else:
                out_ref[role, h] = result
        three_copy(h, role).start()

    def finish(h):
        three_copy(h, 1 - role).wait_recv()
        write_keys(h)

    def cut_piece(slot, at):
        for q in range(sections):
            pieces[q, :, at] = acc[:, slot, q * share:(q + 1) * share].astype(pieces.dtype)

    def send_near_pieces(n):
        for at in range(own)[:1] if n == 0 else range(own)[1:]:
            cut_piece((at + 1) % own, at)

        @pl.when(has_prev)
        def _():
            for d in range(sections):
                near_piece((s + d) % sections, s, n).start()

    def send_pieces():
        send_near_pieces(1)
        for b in range(own, 2 * own):
            cut_piece(b, b)
        for d in range(1, sections):
            own_piece((s + d) % sections, s).start()
        for n in range(n_glob):
            cut_piece(2 * own + n, 2 * own + n)

            @pl.when(is_far(n))
            def _(n=n):
                for d in range(1, sections):
                    far_piece((s + d) % sections, s, n).start()

    def send_far_sums():
        for n in range(n_glob):
            @pl.when(is_far(n))
            def _(n=n):
                total = wide(pieces[s, :, 2 * own + n])
                for d in range(1, sections):
                    origin = (s + d) % sections
                    far_piece(s, origin, n).wait_recv()
                    total += wide(from_far[n, origin])
                far_sum[n] = total.astype(far_sum.dtype)
                farsum_copy(n, p - n * owner_step).start()

    def sum_pieces():
        rows = pl.ds(pl.multiple_of(s * share, share), share)
        total = wide(pieces[s, :, mine])
        for d in range(1, sections):
            origin = (s + d) % sections
            own_piece(s, origin).wait_recv()
            total += wide(from_own[origin])
        acc_share[...] = total

        @pl.when(has_next)
        def _():
            for q in range(sections):
                for n in range(2):
                    near_piece(s, q, n).wait_recv()
            for b in range(own):
                acc_share[:, b] += sum(wide(from_near[q, :, (b + own - 1) % own]) for q in range(sections))
        out_ref[:, heads - 1, 1:own, rows] = acc_share[:, 1:].astype(out_ref.dtype)
        for d in range(1, sections):
            spread_copy((s + d) % sections, s, 0).start()
        for d in spans:
            @pl.when(sends_far(d))
            def _(d=d):
                farsum_copy(0, d).wait_recv()
                acc_share[:, 0] += wide(far_got[d])
        out_ref[:, heads - 1, 0:1, rows] = acc_share[:, 0:1].astype(out_ref.dtype)
        for d in range(1, sections):
            spread_copy((s + d) % sections, s, 1).start()

    def write_keys(h):
        for which, ref in enumerate((dkey_ref, dvalue_ref)):
            ref[pl.ds(h, tok, stride=heads), :] = wide(out_ref[which, h]).reshape(tok, dim)

    for load in loads[2:]:
        load.wait()
    q_wide[...] = wide(q_ref[...])
    g_wide[...] = wide(g_ref[...])
    pass_far(0)
    pass_near(0)
    final = heads - 1

    def head(h):
        one_head = isinstance(h, int) and h == 0
        arrived_far(h)
        arrived_near(h, groups(h)[:2])
        acc[...] = jnp.zeros_like(acc)

        @when(h + 1 < heads)
        def _():
            pass_far(h + 1)
            pass_near(h + 1)

        for k in range(own):
            if k > 0 and one_head:
                arrived_near(h, groups(h)[k + 1:k + 2])
            if k % 2 == 1:
                compute(h, [own - k, own - 1 - k] if one_head else [k - 1, k])
            if k == 0:
                @when(h >= 2)
                def _():
                    swap(h - 2)
            if k == 1:
                @when(h >= 1)
                def _():
                    send_back(h - 1)
            if k == 1 and isinstance(h, int) and h == final:
                send_near_pieces(0)
            if k == own - 1:
                if isinstance(h, int) and h == final:
                    send_pieces()
                else:
                    send_parts(h)

                @when(h >= 2)
                def _():
                    spread(h - 2)

    head(0)

    def middle(h, carry):
        head(h)
        return carry

    lax.fori_loop(1, final, middle, 0)
    head(final)
    swap(final - 1)
    send_far_sums()
    att_ref[...] = att_wide[...].astype(att_ref.dtype)
    for h in range(final - 1):
        finish(h)
    spread(final - 1)
    sum_pieces()
    finish(final - 1)
    for n in range(2):
        for d in range(1, sections):
            spread_copy(s, (s + d) % sections, n).wait_recv()
    write_keys(final)

    def drain(h):
        @pl.when(has_next)
        def _():
            for b, n in groups(h):
                near_copy(h, b, n).wait_send()
        for d in spans:
            @pl.when(sends_far(d))
            def _(d=d):
                far_copy(h, d).wait_send()

        @pl.when(has_prev)
        def _():
            for b, n in groups(h):
                pair_copy(h, b, n, role).wait_send()
        for n in range(n_glob):
            @pl.when(is_far(n))
            def _(n=n):
                for d in range(1, sections):
                    farshare_copy(h, n, (s + d) % sections, s).wait_send()
        if h < final:
            @pl.when(has_prev)
            def _():
                one_copy(h, 1 - role).wait_send()
                back_copy(h).wait_send()
            own_copy(h, 1 - role).wait_send()
            for n in range(n_glob):
                @pl.when(is_far(n))
                def _(n=n):
                    farone_copy(h, n, 1 - role).wait_send()
                    farback_copy(h, n).wait_send()
            for j in range(1, bits):
                two_copy(h, j).wait_send()
            three_copy(h, role).wait_send()

    for h in range(heads):
        drain(h)
    for d in range(sections):
        to = (s + d) % sections

        @pl.when(has_prev)
        def _(to=to):
            for n in range(2):
                near_piece(to, s, n).wait_send()
        for n in range(n_glob):
            @pl.when(is_far(n))
            def _(n=n, to=to, d=d):
                if d > 0:
                    far_piece(to, s, n).wait_send()
                else:
                    farsum_copy(n, p - n * owner_step).wait_send()
        if d > 0:
            own_piece(to, s).wait_send()
            for n in range(2):
                spread_copy(to, s, n).wait_send()


def write_kernel(*refs):
    sems = refs[8]
    copies = [pltpu.make_async_copy(refs[n], refs[4 + n], sems.at[n]) for n in range(4)]
    for c in copies:
        c.start()
    for c in copies:
        c.wait()


def shards(queries, key_states, value_states, out_grad, band_offsets, global_blocks):
    tok, heads, group, dim = queries.shape
    own = tok // BLK
    ctx_count, sections = lax.axis_size("ctx"), lax.axis_size("section")
    bits = sections.bit_length() - 1
    all_blocks = own * ctx_count
    stride_blocks = all_blocks // NGLOB
    n_glob = global_count(all_blocks, stride_blocks, own)
    slots = 2 * own + n_glob
    flat, narrow = (tok * heads * group, dim), (tok * heads, dim)
    hbm, vmem = pl.BlockSpec(memory_space=pltpu.HBM), pl.BlockSpec(memory_space=pltpu.VMEM)

    def low(*lead):
        return pltpu.VMEM((*lead, BLK, dim), jnp.bfloat16)

    def cut(*lead):
        return pltpu.VMEM((*lead, BLK // sections, dim), jnp.bfloat16)

    def full(*shape):
        return pltpu.VMEM(shape, jnp.float32)

    def sems(*dims):
        return [pltpu.SemaphoreType.DMA(dims)] * 2

    results = pl.pallas_call(
        functools.partial(fused_kernel, own, n_glob, stride_blocks // own, ctx_count, bits, dim ** (-0.5), group),
        in_specs=[hbm] * 6,
        out_specs=[vmem] * 4,
        out_shape=[
            jax.ShapeDtypeStruct(flat, jnp.bfloat16),
            jax.ShapeDtypeStruct(flat, jnp.float32),
            jax.ShapeDtypeStruct(narrow, jnp.float32),
            jax.ShapeDtypeStruct(narrow, jnp.float32),
        ],
        scratch_shapes=[
            pltpu.SMEM(band_offsets.shape[::-1], jnp.int32), pltpu.SMEM(global_blocks.shape[::-1], jnp.int32),
            pltpu.VMEM(flat, jnp.bfloat16), pltpu.VMEM(flat, jnp.bfloat16), pltpu.VMEM((2, *narrow), jnp.bfloat16),
            pltpu.SemaphoreType.DMA((6,)),
            full(*narrow), low(2, heads, slots), full(*flat), full(*flat), full(*flat),
            low(2, heads, own), full(2, slots, BLK, dim), full(own, BLK, dim),
            low(2, heads, slots), low(heads, slots), low(heads, own + n_glob), low(heads, own), low(heads, ctx_count),
            low(bits, heads, own), low(bits, heads, own),
            cut(sections, 2, slots), cut(sections, 2, own), cut(sections, 2, own), cut(n_glob, sections, 2),
            cut(n_glob, 2), cut(ctx_count, 2),
            full(2, own, BLK // sections, dim),
            *sems(heads, own), pltpu.SemaphoreType.DMA((heads, ctx_count)), pltpu.SemaphoreType.DMA((heads, n_glob)),
            *sems(heads, own), *sems(heads, n_glob, sections),
            *sems(heads), *sems(heads), *sems(heads, n_glob),
            *sems(heads), pltpu.SemaphoreType.DMA((heads, n_glob)), pltpu.SemaphoreType.DMA((heads, ctx_count)),
            *sems(bits, heads), *sems(heads),
            *sems(sections), *sems(sections, 2),
            *sems(n_glob, sections), pltpu.SemaphoreType.DMA((n_glob,)), pltpu.SemaphoreType.DMA((ctx_count,)),
            *sems(sections, 2),
        ],
        compiler_params=pltpu.CompilerParams(
            vmem_limit_bytes=40 * 2**20, collective_id=0, has_side_effects=True),
    )(*(pltpu.with_memory_space_constraint(x, pltpu.HBM) for x in (
        band_offsets.T, global_blocks.T, queries.reshape(flat), out_grad.reshape(flat),
        key_states.reshape(narrow), value_states.reshape(narrow))))
    att, dq, dkey, dvalue = pl.pallas_call(
        write_kernel,
        in_specs=[vmem] * 4,
        out_specs=[hbm] * 4,
        out_shape=[jax.ShapeDtypeStruct(x.shape, x.dtype) for x in results],
        scratch_shapes=[pltpu.SemaphoreType.DMA((4,))],
        compiler_params=pltpu.CompilerParams(vmem_limit_bytes=2**20),
    )(*results)
    return (att.reshape(queries.shape), dq.reshape(queries.shape), dkey.reshape(key_states.shape),
            dvalue.reshape(key_states.shape))


def solution(mesh):
    wide_spec, narrow_spec = P("ctx", "tp", "section", None), P("ctx", "tp", None)
    return jax.shard_map(
        shards,
        mesh=mesh,
        in_specs=(wide_spec, narrow_spec, narrow_spec, wide_spec, P(), P()),
        out_specs=(wide_spec, wide_spec, narrow_spec, narrow_spec),
        check_vma=False,
    )
```

```python
import functools

import jax
import jax.numpy as jnp
from jax import lax
from jax.experimental import pallas as pl
from jax.experimental.pallas import tpu as pltpu
from jax.sharding import PartitionSpec as P

BLK = 128
NBAND = 3
NGLOB = 4
REACH = ((1, 2), (3, 4))
LOG2E = 1.4426950408889634
LOW = -1e30


def global_count(all_blocks, stride_blocks, own_blocks):
    return len([n for n in range(NGLOB) if n * stride_blocks < all_blocks - 1 - own_blocks])


def dot_nt(a, b):
    return lax.dot_general(a, b, (((1,), (1,)), ((), ())), preferred_element_type=jnp.float32)


def dot_tn(a, b):
    return lax.dot_general(a, b, (((0,), (0,)), ((), ())), preferred_element_type=jnp.float32)


def dot_nn(a, b):
    return lax.dot_general(a, b, (((1,), (0,)), ((), ())), preferred_element_type=jnp.float32)


def when(cond):
    if isinstance(cond, bool):
        return (lambda action: action()) if cond else (lambda action: None)
    return pl.when(cond)


def wide(x):
    return x.astype(jnp.float32)


def block_rows(scale, rows):
    state = [dict() for _ in rows]

    def scores(r, v):
        def selected(block_of):
            parts = [block_of(r["diag"])]
            for off, (reach, near, far) in zip(r["offs"], r["bands"]):
                parts.append(jnp.where(off == reach, block_of(near), block_of(far)))
            return jnp.concatenate(parts + [block_of(slot) for slot in r["globs"]], axis=0)

        v["q"] = r["q"]()
        v["keys"] = selected(r["key_of"])
        v["scores"] = dot_nt(v["keys"], v["q"])
        v["values"] = selected(r["value_of"])

    def softmax(r, v):
        scores = v["scores"]
        width = scores.shape[1]
        key_pos = lax.broadcasted_iota(jnp.int32, (BLK, width), 0)
        query_pos = lax.broadcasted_iota(jnp.int32, (BLK, width), 1) % BLK
        pieces = [jnp.where(key_pos <= query_pos, scores[:BLK], LOW)]
        pieces += [scores[n * BLK:(n + 1) * BLK] for n in range(1, len(r["oks"]) + 1)]
        bias = [jnp.float32(0.0)] + [jnp.where(ok, 0.0, LOW) for ok in r["oks"]]
        top = functools.reduce(jnp.maximum, [jnp.max(x, axis=0, keepdims=True) + b for x, b in zip(pieces, bias)])
        probs = jnp.concatenate(
            [jnp.exp2((x - (top - b)) * (scale * LOG2E)) for x, b in zip(pieces, bias)], axis=0)
        v["share"] = 1.0 / jnp.sum(probs, axis=0, keepdims=True)
        v["probs"], v["low"] = probs, probs.astype(jnp.bfloat16)

    def attend(r, v):
        att = wide((dot_tn(v["values"], v["low"]) * v["share"]).astype(jnp.bfloat16))
        r["put_att"](att.T)
        v["g"] = (wide(r["g"]()).T * v["share"]).astype(jnp.bfloat16)
        v["dots"] = jnp.sum(wide(v["g"]) * att, axis=0, keepdims=True)

    def score_grads(r, v):
        v["ds"] = (v["probs"] * (dot_nn(v["values"], v["g"]) - v["dots"])).astype(jnp.bfloat16)

    def grads(r, v):
        r["put_dq"]((dot_tn(v["keys"], v["ds"]) * scale).T)
        dk, dv = dot_nn(v["ds"], v["q"]) * scale, dot_nt(v["low"], v["g"])
        add = r["add"]
        for which, part in enumerate((dk, dv)):
            def piece(n):
                return part[n * BLK:(n + 1) * BLK]

            add(which, r["diag"], piece(0))
            for m, (off, (reach, near, far)) in enumerate(zip(r["offs"], r["bands"])):
                add(which, near, jnp.where(off == reach, piece(m + 1), 0.0))
                add(which, far, jnp.where(off == reach, 0.0, piece(m + 1)))
            for n, slot in enumerate(r["globs"]):
                add(which, slot, piece(NBAND + n))

    stages = (scores, softmax, attend, score_grads, grads)
    for t in range(len(stages) + len(rows) - 1):
        for n, row in enumerate(rows):
            if 0 <= t - n < len(stages):
                stages[t - n](row, state[n])


def fused_kernel(own, n_glob, owner_step, ctx_count, bits, scale, group, band_hbm, glob_hbm, q_hbm, g_hbm,
                 key_hbm, value_hbm, att_ref, dq_ref, dkey_ref, dvalue_ref,
                 band_ref, glob_ref, q_ref, g_ref, kv_in, load_s, kv_wide, seen, q_wide, g_wide, att_wide,
                 out_ref, acc, acc_own, parts, paired, halves, returned, farback, totals, swapped,
                 pieces, from_own, from_near, from_far, far_sum, far_got, acc_share,
                 near_s, near_r, far_s, far_r, pair_s, pair_r, farpair_s, farpair_r,
                 one_s, one_r, own_s, own_r, farone_s, farone_r, back_s, back_r, farback_s, farback_r,
                 two_s, two_r, three_s, three_r,
                 piece_s, piece_r, nearpiece_s, nearpiece_r, farpiece_s, farpiece_r, farsum_s, farsum_r, spread_s, spread_r):
    sections, share = pieces.shape[0], pieces.shape[-2]
    heads, dim = seen.shape[1], seen.shape[-1]
    tok, lanes = own * BLK, heads * group
    mine = pl.ds(own, own)

    loads = [pltpu.make_async_copy(src, dst, load_s.at[n]) for n, (src, dst) in enumerate((
        (key_hbm, kv_in.at[0]), (value_hbm, kv_in.at[1]), (q_hbm, q_ref), (g_hbm, g_ref),
        (band_hbm, band_ref), (glob_hbm, glob_ref)))]
    for load in loads:
        load.start()
    p, s, parity = lax.axis_index("ctx"), lax.axis_index("section"), lax.axis_index("tp") % 2

    def other(j):
        bit = (1 << (j % bits)) * (1 - parity) + (1 << ((j + 1) % bits)) * parity
        side = (s // bit) % 2
        return s + bit * (1 - 2 * side), side

    mate, role = other(0)
    has_prev, has_next = p > 0, p < ctx_count - 1
    index = p // owner_step

    def owns(at):
        return jnp.logical_and(at % owner_step == 0, at // owner_step < n_glob)

    def sends_far(d):
        return jnp.logical_and(owns(p), p + d < ctx_count)

    def gets_far(d):
        return jnp.logical_and(p - d >= 0, owns(p - d + (p - d < 0) * ctx_count * owner_step))

    spans = range(2, ctx_count)

    def is_far(n):
        return p >= n * owner_step + 2

    def glob_slot(n):
        return jnp.where(p == n * owner_step + 1, 0, 2 * own + n)

    def copy(src, dst, ss, rs, axis, to):
        return pltpu.make_async_remote_copy(src_ref=src, dst_ref=dst, send_sem=ss, recv_sem=rs,
                                            device_id={axis: to}, device_id_type=pl.DeviceIdType.MESH)

    bar = pltpu.get_barrier_semaphore()
    def greet(ctx, section):
        pl.semaphore_signal(bar, inc=1, device_id={"ctx": ctx, "section": section},
                            device_id_type=pl.DeviceIdType.MESH)

    links = [(has_prev, p - 1), (has_next, p + 1)]
    for d in spans:
        links += [(sends_far(d), p + d), (gets_far(d), p - d)]
    for d in range(1, sections):
        greet(p, (s + d) % sections)
    for cond, to in links:
        @pl.when(cond)
        def _(to=to):
            for q in range(sections):
                greet(to, q)
    peers = sections - 1
    for cond, _ in links:
        peers = peers + jnp.where(cond, sections, 0)
    loads[0].wait()
    loads[1].wait()

    def split_heads(which):
        kv_wide[...] = wide(kv_in[which])
        for h in range(heads):
            seen[which, h, mine] = kv_wide[pl.ds(h, tok, stride=heads), :].astype(seen.dtype).reshape(own, BLK, dim)

    split_heads(0)
    split_heads(1)
    pl.semaphore_wait(bar, peers)

    def near_copy(h, b, n):
        return copy(seen.at[role, h, pl.ds(own + b, n)], seen.at[role, h, pl.ds(b, n)],
                    near_s.at[h, b], near_r.at[h, b], "ctx", p + 1)

    def rows_of(slot, h, section):
        return seen.at[:, h, slot, pl.ds(pl.multiple_of(section * share, share), share)]

    def far_copy(h, d):
        return copy(rows_of(own, h, s), rows_of(2 * own + index, h, s), far_s.at[h, d], far_r.at[h, index],
                    "ctx", p + d)

    def far_arrival(h, n):
        return copy(rows_of(own, h, s), rows_of(2 * own + n, h, s), far_s.at[h, 0], far_r.at[h, n], "ctx", p)

    def pair_copy(h, b, n, half):
        blocks = seen.at[half, h, pl.ds(b, n)]
        return copy(blocks, blocks, pair_s.at[h, b], pair_r.at[h, b], "section", mate)

    def farshare_copy(h, n, to, origin):
        rows = rows_of(2 * own + n, h, origin)
        return copy(rows, rows, farpair_s.at[h, n, to], farpair_r.at[h, n, origin], "section", to)

    def one_copy(h, src_half):
        return copy(parts.at[src_half, h, pl.ds(0, own)], paired.at[h, pl.ds(0, own)],
                    one_s.at[h], one_r.at[h], "section", mate)

    def own_copy(h, src_half):
        return copy(parts.at[src_half, h, mine], paired.at[h, mine], own_s.at[h], own_r.at[h], "section", mate)

    def farone_copy(h, n, src_half):
        return copy(parts.at[src_half, h, 2 * own + n], paired.at[h, 2 * own + n],
                    farone_s.at[h, n], farone_r.at[h, n], "section", mate)

    def back_copy(h):
        return copy(halves.at[h, pl.ds(0, own)], returned.at[h], back_s.at[h], back_r.at[h], "ctx", p - 1)

    def farback_copy(h, n):
        return copy(halves.at[h, own + n], farback.at[h, p - n * owner_step], farback_s.at[h, n],
                    farback_r.at[h, p - n * owner_step], "ctx", n * owner_step)

    def farback_arrival(h, d):
        return copy(halves.at[h, own], farback.at[h, d], farback_s.at[h, 0], farback_r.at[h, d], "ctx", p)

    def two_copy(h, j):
        return copy(totals.at[j, h], swapped.at[j, h], two_s.at[j, h], two_r.at[j, h], "section", other(j)[0])

    def three_copy(h, half):
        return copy(out_ref.at[half, h], out_ref.at[half, h], three_s.at[h], three_r.at[h], "section", mate)

    def piece_of(src, dst, ss, rs, ctx, section):
        return pltpu.make_async_remote_copy(src_ref=src, dst_ref=dst, send_sem=ss, recv_sem=rs,
                                            device_id={"ctx": ctx, "section": section},
                                            device_id_type=pl.DeviceIdType.MESH)

    def own_piece(to, origin):
        return piece_of(pieces.at[to, :, mine], from_own.at[origin], piece_s.at[to], piece_r.at[origin], p, to)

    early, late = pl.ds(0, 1), pl.ds(1, own - 1)

    def near_piece(to, origin, n):
        at = (early, late)[n]
        return piece_of(pieces.at[to, :, at], from_near.at[origin, :, at], nearpiece_s.at[to, n],
                        nearpiece_r.at[origin, n], p - 1, to)

    def far_piece(to, origin, n):
        return piece_of(pieces.at[to, :, 2 * own + n], from_far.at[n, origin], farpiece_s.at[n, to],
                        farpiece_r.at[n, origin], p, to)

    def farsum_copy(n, d):
        return copy(far_sum.at[n], far_got.at[d], farsum_s.at[n], farsum_r.at[d], "ctx", n * owner_step)

    def share_of(n, section):
        at = (pl.ds(1, own - 1), pl.ds(0, 1))[n]
        return out_ref.at[:, heads - 1, at, pl.ds(pl.multiple_of(section * share, share), share)]

    def spread_copy(to, origin, n):
        return piece_of(share_of(n, origin), share_of(n, origin), spread_s.at[to, n], spread_r.at[origin, n], p, to)

    first = (0, own - 1)
    rest = tuple(range(own - 2, 0, -1))

    def groups(h):
        return [(b, 1) for b in first + rest] if isinstance(h, int) and h == 0 else [(0, own)]

    for h in range(heads):
        for d in spans:
            @pl.when(sends_far(d))
            def _(h=h, d=d):
                far_copy(h, d).start()

        @pl.when(has_next)
        def _(h=h):
            for b, n in groups(h):
                near_copy(h, b, n).start()

    @pl.when(jnp.logical_not(has_prev))
    def _():
        seen[:, :, :own] = jnp.zeros_like(seen[:, :, :own])
    for n in range(n_glob):
        @pl.when(p < n * owner_step + 1)
        def _(n=n):
            seen[:, :, 2 * own + n] = jnp.zeros_like(seen[:, :, 2 * own + n])

    def pass_far(h):
        for n in range(n_glob):
            @pl.when(is_far(n))
            def _(n=n):
                far_arrival(h, n).wait_recv()
                for d in range(1, sections):
                    farshare_copy(h, n, (s + d) % sections, s).start()

    def pass_near(h):
        @pl.when(has_prev)
        def _():
            for b, n in groups(h):
                near_copy(h, b, n).wait_recv()
                pair_copy(h, b, n, role).start()

    def arrived_far(h):
        for n in range(n_glob):
            @pl.when(is_far(n))
            def _(n=n):
                for d in range(1, sections):
                    farshare_copy(h, n, s, (s + d) % sections).wait_recv()

    def arrived_near(h, blocks):
        @pl.when(has_prev)
        def _():
            for b, n in blocks:
                pair_copy(h, b, n, 1 - role).wait_recv()

    def row_of(h, i):
        row = p * own + i
        spots = [pl.ds(i * (BLK * lanes) + h * group + n, BLK, stride=lanes) for n in range(group)]

        def rows_in(ref):
            return lambda: jnp.concatenate([ref[at, :] for at in spots], axis=0).astype(jnp.bfloat16)

        def put_in(ref):
            def put(x):
                for n, at in enumerate(spots):
                    ref[at, :] = x[n * BLK:(n + 1) * BLK]
            return put

        def block_of(which):
            return lambda slot: seen[which, h, slot]

        def add(which, slot, part):
            acc[which, slot] += part

        offs = [band_ref[1 + m, row] for m in range(NBAND - 1)]
        return dict(offs=offs, oks=[o >= 0 for o in offs] + [glob_ref[n, row] >= 0 for n in range(n_glob)],
                    bands=[(near, own + i - near, own + i - far) for near, far in REACH], diag=own + i,
                    globs=[glob_slot(n) for n in range(n_glob)], q=rows_in(q_wide), g=rows_in(g_wide),
                    key_of=block_of(0), value_of=block_of(1), put_att=put_in(att_wide), put_dq=put_in(dq_ref), add=add)

    def compute(h, rows):
        block_rows(scale, [row_of(h, i) for i in rows])

    def send_parts(h):
        parts[:, h] = acc[...].astype(parts.dtype)

        @pl.when(has_prev)
        def _():
            one_copy(h, 1 - role).start()
        for n in range(n_glob):
            @pl.when(is_far(n))
            def _(n=n):
                farone_copy(h, n, 1 - role).start()
        own_copy(h, 1 - role).start()

    def send_back(h):
        @pl.when(has_prev)
        def _():
            one_copy(h, role).wait_recv()
            near = pl.ds(0, own)
            halves[h, near] = (wide(parts[role, h, near]) + wide(paired[h, near])).astype(halves.dtype)
            back_copy(h).start()
        for n in range(n_glob):
            @pl.when(is_far(n))
            def _(n=n):
                farone_copy(h, n, role).wait_recv()
                at = 2 * own + n
                halves[h, own + n] = (wide(parts[role, h, at]) + wide(paired[h, at])).astype(halves.dtype)
                farback_copy(h, n).start()

    def swap(h):
        own_copy(h, role).wait_recv()
        acc_own[...] = wide(parts[role, h, mine]) + wide(paired[h, mine])

        @pl.when(has_next)
        def _():
            back_copy(h).wait_recv()
            acc_own[...] += wide(returned[h])
        for d in spans:
            @pl.when(sends_far(d))
            def _(d=d):
                farback_arrival(h, d).wait_recv()
                acc_own[0] += wide(farback[h, d])
        totals[1, h] = acc_own[...].astype(totals.dtype)
        two_copy(h, 1).start()

    def spread(h):
        for j in range(1, bits):
            two_copy(h, j).wait_recv()
            result = (wide(totals[j, h]) + wide(swapped[j, h])).astype(totals.dtype)
            if j + 1 < bits:
                totals[j + 1, h] = result
                two_copy(h, j + 1).start()
            else:
                out_ref[role, h] = result
        three_copy(h, role).start()

    def finish(h):
        three_copy(h, 1 - role).wait_recv()
        write_keys(h)

    def cut_piece(slot, at):
        for q in range(sections):
            pieces[q, :, at] = acc[:, slot, q * share:(q + 1) * share].astype(pieces.dtype)

    def send_near_pieces(n):
        for at in range(own)[:1] if n == 0 else range(own)[1:]:
            cut_piece((at + 1) % own, at)

        @pl.when(has_prev)
        def _():
            for d in range(sections):
                near_piece((s + d) % sections, s, n).start()

    def send_pieces():
        send_near_pieces(1)
        for b in range(own, 2 * own):
            cut_piece(b, b)
        for d in range(1, sections):
            own_piece((s + d) % sections, s).start()
        for n in range(n_glob):
            cut_piece(2 * own + n, 2 * own + n)

            @pl.when(is_far(n))
            def _(n=n):
                for d in range(1, sections):
                    far_piece((s + d) % sections, s, n).start()

    def send_far_sums():
        for n in range(n_glob):
            @pl.when(is_far(n))
            def _(n=n):
                total = wide(pieces[s, :, 2 * own + n])
                for d in range(1, sections):
                    origin = (s + d) % sections
                    far_piece(s, origin, n).wait_recv()
                    total += wide(from_far[n, origin])
                far_sum[n] = total.astype(far_sum.dtype)
                farsum_copy(n, p - n * owner_step).start()

    def sum_pieces():
        rows = pl.ds(pl.multiple_of(s * share, share), share)
        total = wide(pieces[s, :, mine])
        for d in range(1, sections):
            origin = (s + d) % sections
            own_piece(s, origin).wait_recv()
            total += wide(from_own[origin])
        acc_share[...] = total

        @pl.when(has_next)
        def _():
            for q in range(sections):
                for n in range(2):
                    near_piece(s, q, n).wait_recv()
            for b in range(own):
                acc_share[:, b] += sum(wide(from_near[q, :, (b + own - 1) % own]) for q in range(sections))
        out_ref[:, heads - 1, 1:own, rows] = acc_share[:, 1:].astype(out_ref.dtype)
        for d in range(1, sections):
            spread_copy((s + d) % sections, s, 0).start()
        for d in spans:
            @pl.when(sends_far(d))
            def _(d=d):
                farsum_copy(0, d).wait_recv()
                acc_share[:, 0] += wide(far_got[d])
        out_ref[:, heads - 1, 0:1, rows] = acc_share[:, 0:1].astype(out_ref.dtype)
        for d in range(1, sections):
            spread_copy((s + d) % sections, s, 1).start()

    def write_keys(h):
        for which, ref in enumerate((dkey_ref, dvalue_ref)):
            ref[pl.ds(h, tok, stride=heads), :] = wide(out_ref[which, h]).reshape(tok, dim)

    for load in loads[2:]:
        load.wait()
    q_wide[...] = wide(q_ref[...])
    g_wide[...] = wide(g_ref[...])
    pass_far(0)
    pass_near(0)
    final = heads - 1

    def head(h):
        one_head = isinstance(h, int) and h == 0
        arrived_far(h)
        arrived_near(h, groups(h)[:2])
        acc[...] = jnp.zeros_like(acc)

        @when(h + 1 < heads)
        def _():
            pass_far(h + 1)
            pass_near(h + 1)

        for k in range(own):
            if k > 0 and one_head:
                arrived_near(h, groups(h)[k + 1:k + 2])
            if k % 2 == 1:
                compute(h, [own - k, own - 1 - k] if one_head else [k - 1, k])
            if k == 0:
                @when(h >= 2)
                def _():
                    swap(h - 2)
            if k == 1:
                @when(h >= 1)
                def _():
                    send_back(h - 1)
            if k == 1 and isinstance(h, int) and h == final:
                send_near_pieces(0)
            if k == own - 1:
                if isinstance(h, int) and h == final:
                    send_pieces()
                else:
                    send_parts(h)

                @when(h >= 2)
                def _():
                    spread(h - 2)

    head(0)

    def middle(h, carry):
        head(h)
        return carry

    lax.fori_loop(1, final, middle, 0)
    head(final)
    swap(final - 1)
    send_far_sums()
    spread(final - 1)
    sum_pieces()
    att_ref[...] = att_wide[...].astype(att_ref.dtype)
    for h in range(final - 1):
        finish(h)
    finish(final - 1)
    for n in range(2):
        for d in range(1, sections):
            spread_copy(s, (s + d) % sections, n).wait_recv()
    write_keys(final)

    def drain(h):
        @pl.when(has_next)
        def _():
            for b, n in groups(h):
                near_copy(h, b, n).wait_send()
        for d in spans:
            @pl.when(sends_far(d))
            def _(d=d):
                far_copy(h, d).wait_send()

        @pl.when(has_prev)
        def _():
            for b, n in groups(h):
                pair_copy(h, b, n, role).wait_send()
        for n in range(n_glob):
            @pl.when(is_far(n))
            def _(n=n):
                for d in range(1, sections):
                    farshare_copy(h, n, (s + d) % sections, s).wait_send()
        if h < final:
            @pl.when(has_prev)
            def _():
                one_copy(h, 1 - role).wait_send()
                back_copy(h).wait_send()
            own_copy(h, 1 - role).wait_send()
            for n in range(n_glob):
                @pl.when(is_far(n))
                def _(n=n):
                    farone_copy(h, n, 1 - role).wait_send()
                    farback_copy(h, n).wait_send()
            for j in range(1, bits):
                two_copy(h, j).wait_send()
            three_copy(h, role).wait_send()

    for h in range(heads):
        drain(h)
    for d in range(sections):
        to = (s + d) % sections

        @pl.when(has_prev)
        def _(to=to):
            for n in range(2):
                near_piece(to, s, n).wait_send()
        for n in range(n_glob):
            @pl.when(is_far(n))
            def _(n=n, to=to, d=d):
                if d > 0:
                    far_piece(to, s, n).wait_send()
                else:
                    farsum_copy(n, p - n * owner_step).wait_send()
        if d > 0:
            own_piece(to, s).wait_send()
            for n in range(2):
                spread_copy(to, s, n).wait_send()


def write_kernel(*refs):
    sems = refs[8]
    copies = [pltpu.make_async_copy(refs[n], refs[4 + n], sems.at[n]) for n in range(4)]
    for c in copies:
        c.start()
    for c in copies:
        c.wait()


def shards(queries, key_states, value_states, out_grad, band_offsets, global_blocks):
    tok, heads, group, dim = queries.shape
    own = tok // BLK
    ctx_count, sections = lax.axis_size("ctx"), lax.axis_size("section")
    bits = sections.bit_length() - 1
    all_blocks = own * ctx_count
    stride_blocks = all_blocks // NGLOB
    n_glob = global_count(all_blocks, stride_blocks, own)
    slots = 2 * own + n_glob
    flat, narrow = (tok * heads * group, dim), (tok * heads, dim)
    hbm, vmem = pl.BlockSpec(memory_space=pltpu.HBM), pl.BlockSpec(memory_space=pltpu.VMEM)

    def low(*lead):
        return pltpu.VMEM((*lead, BLK, dim), jnp.bfloat16)

    def cut(*lead):
        return pltpu.VMEM((*lead, BLK // sections, dim), jnp.bfloat16)

    def full(*shape):
        return pltpu.VMEM(shape, jnp.float32)

    def sems(*dims):
        return [pltpu.SemaphoreType.DMA(dims)] * 2

    results = pl.pallas_call(
        functools.partial(fused_kernel, own, n_glob, stride_blocks // own, ctx_count, bits, dim ** (-0.5), group),
        in_specs=[hbm] * 6,
        out_specs=[vmem] * 4,
        out_shape=[
            jax.ShapeDtypeStruct(flat, jnp.bfloat16),
            jax.ShapeDtypeStruct(flat, jnp.float32),
            jax.ShapeDtypeStruct(narrow, jnp.float32),
            jax.ShapeDtypeStruct(narrow, jnp.float32),
        ],
        scratch_shapes=[
            pltpu.SMEM(band_offsets.shape[::-1], jnp.int32), pltpu.SMEM(global_blocks.shape[::-1], jnp.int32),
            pltpu.VMEM(flat, jnp.bfloat16), pltpu.VMEM(flat, jnp.bfloat16), pltpu.VMEM((2, *narrow), jnp.bfloat16),
            pltpu.SemaphoreType.DMA((6,)),
            full(*narrow), low(2, heads, slots), full(*flat), full(*flat), full(*flat),
            low(2, heads, own), full(2, slots, BLK, dim), full(own, BLK, dim),
            low(2, heads, slots), low(heads, slots), low(heads, own + n_glob), low(heads, own), low(heads, ctx_count),
            low(bits, heads, own), low(bits, heads, own),
            cut(sections, 2, slots), cut(sections, 2, own), cut(sections, 2, own), cut(n_glob, sections, 2),
            cut(n_glob, 2), cut(ctx_count, 2),
            full(2, own, BLK // sections, dim),
            *sems(heads, own), pltpu.SemaphoreType.DMA((heads, ctx_count)), pltpu.SemaphoreType.DMA((heads, n_glob)),
            *sems(heads, own), *sems(heads, n_glob, sections),
            *sems(heads), *sems(heads), *sems(heads, n_glob),
            *sems(heads), pltpu.SemaphoreType.DMA((heads, n_glob)), pltpu.SemaphoreType.DMA((heads, ctx_count)),
            *sems(bits, heads), *sems(heads),
            *sems(sections), *sems(sections, 2),
            *sems(n_glob, sections), pltpu.SemaphoreType.DMA((n_glob,)), pltpu.SemaphoreType.DMA((ctx_count,)),
            *sems(sections, 2),
        ],
        compiler_params=pltpu.CompilerParams(
            vmem_limit_bytes=40 * 2**20, collective_id=0, has_side_effects=True),
    )(*(pltpu.with_memory_space_constraint(x, pltpu.HBM) for x in (
        band_offsets.T, global_blocks.T, queries.reshape(flat), out_grad.reshape(flat),
        key_states.reshape(narrow), value_states.reshape(narrow))))
    att, dq, dkey, dvalue = pl.pallas_call(
        write_kernel,
        in_specs=[vmem] * 4,
        out_specs=[hbm] * 4,
        out_shape=[jax.ShapeDtypeStruct(x.shape, x.dtype) for x in results],
        scratch_shapes=[pltpu.SemaphoreType.DMA((4,))],
        compiler_params=pltpu.CompilerParams(vmem_limit_bytes=2**20),
    )(*results)
    return (att.reshape(queries.shape), dq.reshape(queries.shape), dkey.reshape(key_states.shape),
            dvalue.reshape(key_states.shape))


def solution(mesh):
    wide_spec, narrow_spec = P("ctx", "tp", "section", None), P("ctx", "tp", None)
    return jax.shard_map(
        shards,
        mesh=mesh,
        in_specs=(wide_spec, narrow_spec, narrow_spec, wide_spec, P(), P()),
        out_specs=(wide_spec, wide_spec, narrow_spec, narrow_spec),
        check_vma=False,
    )
```
